256 devices in a mesh: dp: 4 (over y), expert: 64 (over z, x, core).
Axes of the slice: x: 4, y: 4, z: 8, core: 2. Of those that a mesh axis runs over, the one named last changes fastest.
Arguments:
- tokens: bfloat16 [8192, 4096], P('expert'), may hold values from -6 to 6
- out_grad: bfloat16 [8192, 4096], P('expert'), may hold values from -6 to 6
- expert_ids: int32 [8192, 8], P('expert'), may hold values from 0 to 127, all different within a row; in each aligned block of 128 rows (0 to 127, 128 to 255, ...) at most 12 rows name the same one
- combine: bfloat16 [8192, 8], P('expert'), may hold values from 0.049804688 to 0.5
- gate_weight: bfloat16 [64, 768, 4096], P('expert', 'dp'), may hold values from -6 to 6
- up_weight: bfloat16 [64, 768, 4096], P('expert', 'dp'), may hold values from -6 to 6
- down_weight: bfloat16 [64, 768, 4096], P('expert', 'dp'), may hold values from -6 to 6
Outputs:
- input_grad: bfloat16 [8192, 4096], P('expert')
- combine_grad: float32 [8192, 8], P('expert')
- gate_grad: bfloat16 [64, 768, 4096], P('expert', 'dp')
- up_grad: bfloat16 [64, 768, 4096], P('expert', 'dp')
- down_grad: bfloat16 [64, 768, 4096], P('expert', 'dp')
The draws below stay inside these ranges and needn't reach their ends.
Inputs may be any that keep to these rules, and one draw needn't show every extreme that they name: `expert_ids`: each row names 8 different experts. Among the 128 rows of one aligned block no id is named by more than 12 rows, and in some block some id is named by exactly 12.
All inputs are finite; a program needn't handle non-finite values.
Results may differ from the reference program's by a relative error of at most 0.015.
Values may be sent and summed in bfloat16 or wider, within the bound.
No kernel may reach another device: no remote copies, remote signals or barrier semaphores. Data moves between devices by JAX's collectives and lax.ppermute only.
A program may use at most 128 MiB of HBM per device.

```python
import math
from functools import partial
import jax
import jax.numpy as jnp
import numpy as np
from jax import lax

D = 4096
FF = 1536
ROUTED = 128
TOP = 8
TOK_DEV = 128
CAP = 12
EXPERTS = 32
TOKENS = 8192
BATCH = 512
N_DP = 4


def level_of(rng, shape, shards, low, largest):
    gain, own = 1.0, jax.random.fold_in(rng, 6)
    for axis_at, shards_of in shards:
        steps = jnp.exp(jax.random.uniform(jax.random.fold_in(own, axis_at), (shards_of,), jnp.float32, low / len(shards), largest / len(shards)))
        gain = gain * jnp.repeat(steps, shape[axis_at] // shards_of).reshape([-1 if axis == axis_at else 1 for axis in range(len(shape))])
    return gain


def deal_out(stream_key, own, number, rows, amount, top, limit, skew):
    sequence = jax.random.permutation(stream_key, amount)
    crowded, ordinary = load_shares(amount, rows * top, limit, skew, True), load_shares(amount, rows * top, limit, skew, False)
    places = jnp.arange(amount)

    def named(lengths, turn):
        used = int((lengths > 0).sum())
        fixed = max(1, used // 4)
        passed = fixed + (places - fixed + turn * (used - fixed)) % max(1, amount - fixed)
        return jnp.zeros((amount,), jnp.int32).at[sequence[jnp.where(places < fixed, places, passed)]].set(jnp.asarray(lengths, jnp.int32))

    lengths = jnp.where(number % 4 == 0, named(crowded, number // 4), named(ordinary, number - number // 4 - 1))
    mixed = jax.random.permutation(jax.random.fold_in(own, 3), amount)
    donor, receiver = mixed[0:amount // 2 * 2:2], mixed[1:amount // 2 * 2:2]
    slack = jnp.minimum(lengths[donor] - 1, limit - lengths[receiver]) // 2
    slack = jnp.where((donor == sequence[0]) | (receiver == sequence[0]) | (lengths[receiver] == 0), 0, jnp.maximum(slack, 0))
    passed = jax.random.randint(jax.random.fold_in(own, 4), (amount // 2,), 0, 1 << 20) % (slack + 1)
    lengths = lengths.at[donor].add(-passed).at[receiver].add(passed)
    items = jnp.searchsorted(jnp.cumsum(lengths), jnp.arange(rows * top), side="right").astype(jnp.int32)
    listing = items.reshape(top, rows).T
    listing = listing[jax.random.permutation(jax.random.fold_in(own, 1), rows)]
    turn = jax.random.randint(jax.random.fold_in(own, 2), (rows, 1), 0, top)
    return jnp.take_along_axis(listing, (jnp.arange(top)[None, :] + turn) % top, axis=1)


def load_shares(count, total, limit, skew, full):
    portions = [(1 << 20) // math.isqrt(standing ** skew) + 1 for standing in range(1, count + 1)]
    largest = limit if full else min(limit, max(-(-total // count), total * portions[0] // sum(portions)))
    least = 1 if total - largest >= count - 1 else 0
    holding, rest = [largest] + [least] * (count - 1), total - largest - least * (count - 1)
    while rest > 0:
        candidates = [i for i in range(1, count) if holding[i] < largest] or [i for i in range(1, count) if holding[i] < limit]
        mass, left = sum([portions[i] for i in candidates]), rest
        for i in candidates:
            more = min(limit - holding[i], max(1, left * portions[i] // mass), rest)
            holding[i] = holding[i] + more
            rest = rest - more
    return np.array(holding)


def centred(rng, extent, spread, most, cuts=(), held_as=jnp.bfloat16):
    array = jax.random.normal(rng, extent, jnp.float32) * spread
    if len(cuts) > 0:
        array = level_of(rng, extent, cuts, -0.22, 0.18) * array
    return jnp.clip(array, min=-most, max=most).astype(held_as)


def setup_inputs(seed: int = 0) -> dict:
    keys = jax.random.split(jax.random.key(seed), 8)
    tokens = centred(keys[0], (TOKENS, D), 1.0, 6.0, ((0, 64),))
    out_grad = centred(keys[1], (TOKENS, D), 1.0, 6.0, ((0, 64),))
    expert_ids_keys = jax.random.split(jax.random.fold_in(keys[2], 1), TOKENS // TOK_DEV)
    expert_ids_turns = jax.random.permutation(jax.random.fold_in(keys[2], 3), TOKENS // TOK_DEV)
    expert_ids = jax.vmap(lambda own, number: deal_out(jax.random.fold_in(keys[2], 2), own, number, TOK_DEV, ROUTED, TOP, CAP, 2))(expert_ids_keys, expert_ids_turns).reshape((TOKENS, TOP))
    combine = jnp.clip(jnp.exp(math.log(0.5) - 2.306499 * jax.random.uniform(keys[3], (TOKENS, TOP), jnp.float32) ** level_of(keys[3], (TOKENS, TOP), ((0, 64),), -0.2, 0.2)), 0.049804688, 0.5).astype(jnp.bfloat16)
    gate_weight = centred(keys[4], (2 * EXPERTS, FF // 2, D), 1.0, 6.0, ((0, 64), (1, 4)))
    up_weight = centred(keys[5], (2 * EXPERTS, FF // 2, D), 1.0, 6.0, ((0, 64), (1, 4)))
    down_weight = centred(keys[6], (2 * EXPERTS, FF // 2, D), 1.0, 6.0, ((0, 64), (1, 4)))
    return dict(tokens=tokens, out_grad=out_grad, expert_ids=expert_ids, combine=combine, gate_weight=gate_weight, up_weight=up_weight, down_weight=down_weight)


def slot_table(routes, weights_in, experts):
    expert_list = jnp.arange(experts, dtype=jnp.int32)
    matches = routes[:, :, None] == expert_list[None, None, :]
    member = jnp.sum(matches.astype(jnp.int32), axis=1).astype(jnp.int32)
    weight_of = jnp.sum(jnp.where(matches, weights_in.astype(jnp.float32)[:, :, None], jnp.float32(0.0)), axis=1)
    rank_of = (jnp.cumsum(member, axis=0) - 1).astype(jnp.int32)
    slot_ids = jnp.arange(CAP, dtype=jnp.int32)
    placed = (member.T[:, None, :] == 1) & (rank_of.T[:, None, :] == slot_ids[None, :, None])
    placed = placed.astype(jnp.float32)
    slot_weight = jnp.sum(placed * weight_of.T[:, None, :], axis=2)
    return placed, slot_weight


def reference(tokens, out_grad, expert_ids, combine, gate_weight, up_weight, down_weight):
    experts = gate_weight.shape[0] // 2
    blocks = tokens.shape[0] // TOK_DEV
    groups = 2 * N_DP
    group_width = FF // groups
    highest = lax.Precision.HIGHEST
    route_blocks = expert_ids.reshape(blocks, TOK_DEV, TOP)
    weight_blocks = combine.reshape(blocks, TOK_DEV, TOP)
    placed, slot_weight = jax.vmap(partial(slot_table, experts=experts))(route_blocks, weight_blocks)
    placed = jnp.transpose(placed, (1, 0, 2, 3))
    slot_weight = jnp.transpose(slot_weight, (1, 0, 2))
    token_blocks = tokens.reshape(blocks, TOK_DEV, D).astype(jnp.float32)
    grad_blocks = out_grad.reshape(blocks, TOK_DEV, D).astype(jnp.float32)
    gate_all = gate_weight.reshape(experts, FF, D)
    up_all = up_weight.reshape(experts, FF, D)
    down_all = down_weight.reshape(experts, FF, D)
    contract = (((1,), (1,)), ((), ()))
    rows_first = (((0,), (0,)), ((), ()))
    factor = float(BATCH) ** -0.5

    def expert_step(carried, inputs):
        input_acc, combine_acc = carried
        place_e, weight_e, gate_w, up_w, down_w, expert = inputs
        token_rows = jnp.einsum("bct,btd->bcd", place_e, token_blocks, precision=highest).astype(jnp.bfloat16).reshape(-1, D)
        grad_rows = jnp.einsum("bct,btd->bcd", place_e, grad_blocks, precision=highest).astype(jnp.bfloat16).reshape(-1, D)
        row_weight = weight_e.reshape(-1)
        gate_pre = lax.dot_general(token_rows, gate_w, contract, preferred_element_type=jnp.float32) * D ** -0.5
        up_pre = lax.dot_general(token_rows, up_w, contract, preferred_element_type=jnp.float32) * D ** -0.5
        back_proj = lax.dot_general(grad_rows, down_w, contract, preferred_element_type=jnp.float32)
        sigmoid = jax.nn.sigmoid(gate_pre)
        active = gate_pre * sigmoid
        hidden = active * up_pre
        slope_of = sigmoid * (1.0 + gate_pre * (1.0 - sigmoid))
        scaled = row_weight[:, None] * back_proj * D ** -0.5
        grad_gate = (scaled * up_pre * slope_of).astype(jnp.bfloat16)
        grad_up = (scaled * active).astype(jnp.bfloat16)
        weighted = (row_weight[:, None] * hidden).astype(jnp.bfloat16)
        gate_groups = gate_w.astype(jnp.float32).reshape(groups, group_width, D)
        up_groups = up_w.astype(jnp.float32).reshape(groups, group_width, D)
        input_terms = jnp.einsum("rgs,gsd->grd", grad_gate.astype(jnp.float32).reshape(-1, groups, group_width), gate_groups, precision=highest)
        input_terms = input_terms + jnp.einsum("rgs,gsd->grd", grad_up.astype(jnp.float32).reshape(-1, groups, group_width), up_groups, precision=highest)
        input_terms = lax.optimization_barrier((input_terms * (2 * FF) ** -0.5).astype(jnp.bfloat16))
        input_rows = jnp.sum(input_terms.astype(jnp.float32), axis=0)
        combine_terms = jnp.sum((hidden * back_proj).reshape(-1, groups, group_width), axis=2) * (D * FF) ** -0.5
        combine_terms = lax.optimization_barrier(combine_terms.astype(jnp.bfloat16))
        combine_rows = jnp.sum(combine_terms.astype(jnp.float32), axis=1)
        input_acc = input_acc + jnp.einsum("bct,bcd->btd", place_e, input_rows.reshape(blocks, CAP, D), precision=highest)
        token_weight = jnp.einsum("bct,bc->bt", place_e, combine_rows.reshape(blocks, CAP), precision=highest)
        combine_acc = combine_acc + (route_blocks == expert).astype(jnp.float32) * token_weight[:, :, None]
        wgrad_gate = (lax.dot_general(grad_gate, token_rows, rows_first, preferred_element_type=jnp.float32) * factor).astype(jnp.bfloat16)
        wgrad_up = (lax.dot_general(grad_up, token_rows, rows_first, preferred_element_type=jnp.float32) * factor).astype(jnp.bfloat16)
        wgrad_down = (lax.dot_general(weighted, grad_rows, rows_first, preferred_element_type=jnp.float32) * factor).astype(jnp.bfloat16)
        return (input_acc, combine_acc), (wgrad_gate, wgrad_up, wgrad_down)

    start = (jnp.zeros((blocks, TOK_DEV, D), jnp.float32), jnp.zeros((blocks, TOK_DEV, TOP), jnp.float32))
    scanned = (placed, slot_weight, gate_all, up_all, down_all, jnp.arange(experts, dtype=jnp.int32))
    (input_acc, combine_acc), (gate_grads, up_grads, down_grads) = lax.scan(expert_step, start, scanned)
    shape_out = (2 * experts, FF // 2, D)
    return (input_acc.reshape(-1, D).astype(jnp.bfloat16), combine_acc.reshape(-1, TOP), gate_grads.reshape(shape_out), up_grads.reshape(shape_out), down_grads.reshape(shape_out))
```

```python
import jax
import jax.numpy as jnp
from jax import lax
from jax.experimental import pallas as pl
from jax.experimental.pallas import tpu as pltpu
from jax.sharding import PartitionSpec as P

D = 4096
FF = 1536
ROUTED = 128
TOP = 8
CAP = 12
BF = jnp.bfloat16
F32 = jnp.float32
I32 = jnp.int32
HALF = D // 2
CH = 512
NT = (((1,), (1,)), ((), ()))
NN = (((1,), (0,)), ((), ()))
TN = (((0,), (0,)), ((), ()))
OFFS = (0, -1, 1, 2)

SMEM = pl.BlockSpec(memory_space=pltpu.SMEM)
VMEM = pl.BlockSpec(memory_space=pltpu.VMEM)


def mm(a, b, dims=NN):
    return lax.dot_general(a, b, dims, preferred_element_type=F32)


def iota(shape, axis):
    return lax.broadcasted_iota(I32, shape, axis)


def onehot(mask):
    return jnp.where(mask, F32(1.0), F32(0.0))


def call(body, outs, args, scratch=(), specs=None, out_specs=None, name=None):
    return pl.pallas_call(
        body,
        out_shape=[jax.ShapeDtypeStruct(s, t) for s, t in outs],
        in_specs=specs or [SMEM] + [VMEM] * (len(args) - 1),
        out_specs=out_specs or [VMEM] * len(outs),
        scratch_shapes=list(scratch),
        compiler_params=pltpu.CompilerParams(vmem_limit_bytes=60 * 1024 * 1024),
        name=name,
    )(*args)


def chunk_cols(y, off, width=CH):
    return pl.ds(pl.multiple_of(lax.rem(y + (off + 4), 4) * width, width), width)


def slot_key(ids):
    e = iota((32, 128), 0)
    member = jnp.zeros((32, 128), F32)
    for k in range(TOP):
        member = member + onehot(ids[k : k + 1, :] == e)
    upto = onehot(iota((128, 128), 0) <= iota((128, 128), 1)).astype(BF)
    rank = mm(member.astype(BF), upto) - 1.0
    return jnp.where(member > 0.5, rank, F32(-1.0))


def spread_rows():
    return onehot(iota((512, 32), 0) // 16 == iota((512, 32), 1)).astype(BF)


def own_columns(ref, y):
    low = ref[:, chunk_cols(y, 0)]
    high = ref[:, pl.ds(pl.multiple_of(HALF + y * CH, CH), CH)]
    return low, high


def send_first_body(pos, ids, tokens, p1):
    y = pos[0]
    key = mm(spread_rows(), slot_key(ids[...]).astype(BF))
    r = iota((512, 128), 0)
    high = (r // 8) % 2 == 1
    m8 = key == (r % 8).astype(F32)
    lhs = jnp.concatenate([onehot(m8 & ~high), onehot(m8 & high)], axis=1).astype(BF)
    rhs = jnp.concatenate(own_columns(tokens, y), axis=0)
    p1[...] = mm(lhs, rhs).astype(BF)


def send_rest_body(pos, ids, comb, tokens, grads, p2, p3):
    y = pos[0]
    idv = ids[...]
    e = iota((32, 128), 0)
    wt = jnp.zeros((32, 128), F32)
    for k in range(TOP):
        wt = wt + jnp.where(idv[k : k + 1, :] == e, comb[k : k + 1, :].astype(F32), F32(0.0))
    rows = spread_rows()
    key = mm(rows, slot_key(idv).astype(BF))
    wt = mm(rows, wt.astype(BF))
    r = iota((512, 128), 0)
    high = (r // 8) % 2 == 1
    second = (r // 4) % 2 == 1
    m8 = key == (r % 8).astype(F32)
    m4 = key == (8 + r % 4).astype(F32)
    g_low, g_high = own_columns(grads, y)
    x_low, x_high = own_columns(tokens, y)
    lhs = jnp.concatenate([onehot(m8 & ~high), onehot(m8 & high)], axis=1).astype(BF)
    p2[:, :CH] = mm(lhs, jnp.concatenate([g_low, g_high], axis=0)).astype(BF)
    lane = iota((128, 128), 1)
    w8 = (onehot(m8) * wt).astype(BF)
    w4 = (onehot(m4) * wt).astype(BF)
    wb = mm(w8, onehot(lane < 64).astype(BF)) + mm(w4, onehot(lane >= 64).astype(BF))
    p2[:, CH:] = wb.astype(BF)
    lhs = jnp.concatenate(
        [
            onehot(m4 & ~high & ~second),
            onehot(m4 & high & ~second),
            onehot(m4 & ~high & second),
            onehot(m4 & high & second),
        ],
        axis=1,
    ).astype(BF)
    rhs = jnp.concatenate([x_low, x_high, g_low, g_high], axis=0)
    p3[...] = mm(lhs, rhs).astype(BF)


def weight_send_body(pos, gw, uw, dw, out):
    other = pl.ds(pl.multiple_of((1 - pos[1]) * HALF, HALF), HALF)
    for m, w in enumerate((gw, uw, dw)):
        out[m] = w[:, other]


def weight_join_body(pos, gw, uw, dw, got, out):
    h = pos[1]
    mine = pl.ds(pl.multiple_of(h * HALF, HALF), HALF)
    own = pl.ds(pl.multiple_of(h * 192, 192), 192)
    other = pl.ds(pl.multiple_of((1 - h) * 192, 192), 192)
    for m, w in enumerate((gw, uw, dw)):
        out[m, own, :] = w[:, mine]
        out[m, other, :] = got[m]


def gate_up_body(pos, x0, x1, x2, x3, w, out):
    y = pos[0]
    for m in range(2):
        acc = None
        for x, off in zip((x0, x1, x2, x3), OFFS):
            part = mm(x[...], w[m, :, chunk_cols(y, off)], NT)
            acc = part if acc is None else acc + part
        out[:, m * 384 : (m + 1) * 384] = acc


def back_body(pos, x0, x1, x2, x3, w, out):
    y = pos[0]
    acc = None
    for x, off in zip((x0, x1, x2, x3), OFFS):
        part = mm(x[...], w[2, :, chunk_cols(y, off)], NT)
        acc = part if acc is None else acc + part
    out[...] = acc


def mixed_body(pos, x0, x1, x2, x3, w, out):
    y = pos[0]
    accs = [None] * 3
    for x, off in zip((x0, x1, x2, x3), OFFS):
        for m in range(3):
            part = mm(x[...], w[m, :, chunk_cols(y, off)], NT)
            accs[m] = part if accs[m] is None else accs[m] + part
    second = (iota((512, 384), 0) // 4) % 2 == 1
    out[:, :384] = jnp.where(second, accs[2], accs[0])
    out[:, 384:] = accs[1]


def hidden_math(gate, up, back, w):
    scale = D**-0.5
    gate = gate * scale
    up = up * scale
    sig = jax.nn.sigmoid(gate)
    active = gate * sig
    hidden = active * up
    slope = sig * (1.0 + gate * (1.0 - sig))
    scaled = w * back * scale
    return scaled * up * slope, scaled * active, w * hidden, hidden * back


def own_units(h, rows):
    return (iota((rows, 384), 1) >= 192) == (h == 1)


def combine_term(product, h):
    rows = product.shape[0]
    part = jnp.sum(jnp.where(own_units(h, rows), product, F32(0.0)), axis=1, keepdims=True)
    return jnp.broadcast_to(part * (D * FF) ** (-0.5), (rows, 128))


def mid8_body(
    pos, gu_a, gu_b, bk_a, bk_b, wb, w,
    gg, gu, wt, cb, d0a, d0b, dpa, dpb, dma, dmb, d2a, d2b,
):
    y, h = pos[0], pos[1]
    for i in range(4):
        rs = pl.ds(i * 128, 128)
        g, u, a, hb = hidden_math(
            gu_a[rs, :384] + gu_b[rs, :384],
            gu_a[rs, 384:] + gu_b[rs, 384:],
            bk_a[rs, :] + bk_b[rs, :],
            wb[rs, 0:1].astype(F32),
        )
        gg[rs, :] = g.astype(BF)
        gu[rs, :] = u.astype(BF)
        wt[rs, :] = a.astype(BF)
        cb[rs, :] = combine_term(hb, h).astype(BF)
    for off, (top, bottom) in ((2, (d2a, d2b)), (1, (dpa, dpb)), (-1, (dma, dmb)), (0, (d0a, d0b))):
        cols = chunk_cols(y, off)
        full = mm(gg[...], w[0, :, cols]) + mm(gu[...], w[1, :, cols])
        full = (full * (2 * FF) ** (-0.5)).astype(BF)
        top[...] = full[:256]
        bottom[...] = full[256:]


def mid4_body(
    pos, mx_a, mx_b, wb, cb8, w,
    gg, gu, wt, cb, d0a, d0b, dpa, dpb, dma, dmb, d2a, d2b, gg_s, gu_s,
):
    y, h = pos[0], pos[1]
    second = (iota((128, 384), 0) // 4) % 2 == 1
    lane = iota((128, 128), 1)
    for i in range(4):
        rs = pl.ds(i * 128, 128)
        mix = mx_a[rs, :384] + mx_b[rs, :384]
        up = mx_a[rs, 384:] + mx_b[rs, 384:]
        gate = jnp.where(second, pltpu.roll(mix, 4, 0), mix)
        back = jnp.where(second, mix, pltpu.roll(mix, 124, 0))
        up = jnp.where(second, pltpu.roll(up, 4, 0), up)
        g, u, a, hb = hidden_math(gate, up, back, wb[rs, 64:65].astype(F32))
        gg_s[rs, :] = g.astype(BF)
        gu_s[rs, :] = u.astype(BF)
        gg[rs, :] = jnp.where(second, F32(0.0), g).astype(BF)
        gu[rs, :] = jnp.where(second, F32(0.0), u).astype(BF)
        wt[rs, :] = jnp.where(second, a, F32(0.0)).astype(BF)
        c8 = cb8[rs, :].astype(F32)
        cb[rs, :] = jnp.where(lane < 64, c8, combine_term(hb, h)).astype(BF)
    second = (iota((512, 256), 0) // 4) % 2 == 1
    for off, (top, bottom) in ((2, (d2a, d2b)), (1, (dpa, dpb)), (-1, (dma, dmb)), (0, (d0a, d0b))):
        cols = chunk_cols(y, off)
        full = mm(gg_s[...], w[0, :, cols]) + mm(gu_s[...], w[1, :, cols])
        part = jnp.where(second, full[:, 256:], full[:, :256])
        part = (part * (2 * FF) ** (-0.5)).astype(BF)
        top[...] = part[:256]
        bottom[...] = part[256:]


def sum3(a, b, c):
    return (a[...].astype(F32) + b[...].astype(F32) + c[...].astype(F32)).astype(BF)


def finish8_body(d0a, d0b, ma, mb, pa, pb, out):
    out[:256, :] = sum3(d0a, ma, pa)
    out[256:, :] = sum3(d0b, mb, pb)


def finish4_body(d0a, d0b, ma, mb, pa, pb, cb, out):
    out[:256, :256] = sum3(d0a, ma, pa)
    out[256:, :256] = sum3(d0b, mb, pb)
    out[:, 256:] = cb[...]


def wgrad_parts(t, rows, xs, gs, ms, m):
    factor = 512.0 ** (-0.5)
    for x, mix, off in zip(gs if m == 2 else xs, ms, OFFS):
        part = mm(t[m, rows, :512], x[...]) + mm(t[m, rows, 512:], mix[...])
        yield off, (part * factor).astype(BF)


def wgrad_other_body(pos, g8, u8, w8, g4, u4, w4, *refs):
    xs, gs, ms, (t, out) = refs[:4], refs[4:8], refs[8:12], refs[12:]
    y, h = pos[0], pos[1]
    for m, (a, b) in enumerate(((g8, g4), (u8, u4), (w8, w4))):
        t[m, :, :512] = a[...].T
        t[m, :, 512:] = b[...].T
    other = pl.ds(pl.multiple_of((1 - h) * 192, 192), 192)
    for m in range(3):
        for off, part in wgrad_parts(t, other, xs, gs, ms, m):
            out[m, :, chunk_cols(y, off)] = part


def wgrad_own_body(pos, t, got, *refs):
    xs, gs, ms, outs = refs[:4], refs[4:8], refs[8:12], refs[12:]
    y, h = pos[0], pos[1]
    own = pl.ds(pl.multiple_of(h * 192, 192), 192)
    for m in range(3):
        outs[m][:, pl.ds(pl.multiple_of((1 - h) * HALF, HALF), HALF)] = got[m]
        for off, part in wgrad_parts(t, own, xs, gs, ms, m):
            col = h * HALF + lax.rem(y + (off + 4), 4) * CH
            outs[m][:, pl.ds(pl.multiple_of(col, CH), CH)] = part


def collect_body(ids, r1, r3, qa, qb, cg):
    idv = ids[...]
    key = slot_key(idv)
    rows = spread_rows()
    keyt = mm(key.T.astype(BF), rows, NT)
    c = iota((128, 512), 1)
    high = (c // 8) % 2 == 1
    second = (c // 4) % 2 == 1
    m8 = keyt == (c % 8).astype(F32)
    m4 = keyt == (8 + c % 4).astype(F32)
    b1, b3 = r1[...], r3[:, :256]
    for q, half in ((qa, ~high), (qb, high)):
        o = mm(onehot(m8 & half).astype(BF), b1)
        lo = mm(onehot(m4 & half & ~second).astype(BF), b3)
        hi = mm(onehot(m4 & half & second).astype(BF), b3)
        q[:, :256] = (o[:, :256] + lo).astype(BF)
        q[:, 256:] = (o[:, 256:] + hi).astype(BF)
    key = mm(rows, key.astype(BF))
    r = iota((512, 128), 0)
    c8 = jnp.broadcast_to(r3[:, 256:257].astype(F32), (512, 128))
    c4 = jnp.broadcast_to(r3[:, 320:321].astype(F32), (512, 128))
    z = jnp.where(key == (r % 8).astype(F32), c8, F32(0.0))
    z = z + jnp.where((key == (8 + r % 4).astype(F32)) & ((r // 4) % 2 == 0), c4, F32(0.0))
    tokw = mm(rows, z.astype(BF), TN)
    e = iota((32, 128), 0)
    for k in range(TOP):
        cg[k : k + 1, :] = jnp.sum(
            jnp.where(idv[k : k + 1, :] == e, tokw, F32(0.0)), axis=0, keepdims=True
        )


def assemble_body(pos, *refs):
    qs, out = refs[:8], refs[8]
    y = pos[0]
    for i, off in enumerate(OFFS):
        c = lax.rem(y + (off + 4), 4) * CH
        out[:, pl.ds(pl.multiple_of(c, CH), CH)] = qs[2 * i][...]
        out[:, pl.ds(pl.multiple_of(HALF + c, CH), CH)] = qs[2 * i + 1][...]


def on_device(tokens, out_grad, expert_ids, combine, gate_weight, up_weight, down_weight):
    n_dp = lax.axis_size("dp")
    width = lax.axis_size("expert")
    up_ring = [(i, (i + 1) % n_dp) for i in range(n_dp)]
    down_ring = [(i, (i - 1) % n_dp) for i in range(n_dp)]
    across = [(i, (i + 2) % n_dp) for i in range(n_dp)]
    cores = [(i, i ^ 1) for i in range(width)]

    def up(x):
        return lax.ppermute(x, "dp", up_ring)

    def down(x):
        return lax.ppermute(x, "dp", down_ring)

    def swap(x):
        return lax.ppermute(x, "expert", cores)

    def exchange(x):
        n = x.shape[1]
        x = x.reshape(width, 8, n)
        return lax.all_to_all(x, "expert", split_axis=0, concat_axis=0, tiled=True).reshape(-1, n)

    pos = jnp.stack([lax.axis_index("dp"), lax.axis_index("expert") % 2]).astype(I32)
    ids = expert_ids.T
    comb = combine.T
    gw, uw, dw = gate_weight[0], up_weight[0], down_weight[0]

    (p1,) = call(send_first_body, [((512, CH), BF)], (pos, ids, tokens), name="send_first")
    p1 = exchange(p1)
    p2, p3 = call(
        send_rest_body,
        [((512, CH + 128), BF), ((512, CH), BF)],
        (pos, ids, comb, tokens, out_grad),
        name="send_rest",
    )
    p2 = exchange(p2)
    p3 = exchange(p3)

    (wsend,) = call(
        weight_send_body, [((3, 192, HALF), BF)], (pos, gw, uw, dw), name="weight_send"
    )
    wgot = swap(wsend)
    (wall,) = call(
        weight_join_body, [((3, 384, HALF), BF)], (pos, gw, uw, dw, wgot), name="weight_join"
    )

    xl, xr = up(p1), down(p1)
    xo = up(xl)
    xs = (p1, xl, xr, xo)
    wb = p2[:, CH:]
    p2 = p2[:, :CH]
    gl, gr = up(p2), down(p2)
    go = down(gr)
    gs = (p2, gl, gr, go)
    ml, mr = up(p3), down(p3)
    mo = jnp.concatenate([up(ml[:256]), down(mr[256:])], axis=0)
    ms = (p3, ml, mr, mo)

    (gu_a,) = call(gate_up_body, [((512, 768), F32)], (pos, *xs, wall), name="gate_up")
    gu_b = swap(gu_a)
    (bk_a,) = call(back_body, [((512, 384), F32)], (pos, *gs, wall), name="back")
    bk_b = swap(bk_a)
    unit_rows = [((512, 384), BF)] * 3 + [((512, 128), BF)]
    g8, u8, w8, cb8, d0a, d0b, dpa, dpb, dma, dmb, d2a, d2b = call(
        mid8_body, unit_rows + [((256, CH), BF)] * 8,
        (pos, gu_a, gu_b, bk_a, bk_b, wb, wall), name="mid8",
    )

    def ring_sum(dpa, dpb, dma, dmb, d2a, d2b):
        pa, mb = up(d2a), down(d2b)
        pb, ma = up(dpb), down(dma)
        return ma, down(dmb + mb), up(dpa + pa), pb

    ma, mb, pa, pb = ring_sum(dpa, dpb, dma, dmb, d2a, d2b)
    (r1,) = call(
        finish8_body, [((512, CH), BF)], (d0a, d0b, ma, mb, pa, pb),
        specs=[VMEM] * 6, name="finish8",
    )
    r1 = exchange(r1)

    (mx_a,) = call(mixed_body, [((512, 768), F32)], (pos, *ms, wall), name="mixed")
    mx_b = swap(mx_a)
    g4, u4, w4, cb, d0a, d0b, dpa, dpb, dma, dmb, d2a, d2b = call(
        mid4_body, unit_rows + [((256, CH // 2), BF)] * 8, (pos, mx_a, mx_b, wb, cb8, wall),
        scratch=[pltpu.VMEM((512, 384), BF)] * 2, name="mid4",
    )
    ma, mb, pa, pb = ring_sum(dpa, dpb, dma, dmb, d2a, d2b)
    (r3,) = call(
        finish4_body, [((512, 384), BF)], (d0a, d0b, ma, mb, pa, pb, cb),
        specs=[VMEM] * 7, name="finish4",
    )
    r3 = exchange(r3)

    t, dsend = call(
        wgrad_other_body, [((3, 384, 1024), BF), ((3, 192, HALF), BF)],
        (pos, g8, u8, w8, g4, u4, w4, *xs, *gs, *ms), name="wgrad_other",
    )
    dgot = swap(dsend)
    dwg, dwu, dwd = call(
        wgrad_own_body, [((192, D), BF)] * 3, (pos, t, dgot, *xs, *gs, *ms), name="wgrad_own"
    )

    qa, qb, cg = call(
        collect_body, [((128, CH), BF)] * 2 + [((TOP, 128), F32)], (ids, r1, r3),
        specs=[VMEM] * 3, name="collect",
    )
    cg = cg + up(cg) + down(cg) + lax.ppermute(cg, "dp", across)
    la, rb = up(qa), down(qb)
    lb, ra = up(qb), down(qa)
    oa, ob = up(la), down(rb)
    (input_grad,) = call(
        assemble_body, [((128, D), BF)], (pos, qa, qb, la, lb, ra, rb, oa, ob), name="assemble"
    )
    return (input_grad, cg.T, dwg[None], dwu[None], dwd[None])


def solution(mesh):
    rows = P("expert", None)
    units = P("expert", "dp", None)
    return jax.shard_map(
        on_device,
        mesh=mesh,
        in_specs=(rows, rows, rows, rows, units, units, units),
        out_specs=(rows, rows, units, units, units),
        check_vma=False,
    )
```

```python
import functools

import jax
import jax.numpy as jnp
from jax import lax
from jax.experimental import pallas as pl
from jax.experimental.pallas import tpu as pltpu
from jax.sharding import PartitionSpec as P

D = 4096
FF = 1536
TOP = 8
EXPERTS = 32
BF = jnp.bfloat16
F32 = jnp.float32
I32 = jnp.int32
HALF = D // 2
CH = 512
CAP = 12
GROUP = 2 * CAP
ROWS = EXPERTS * GROUP
UNITS = 384
NT = (((1,), (1,)), ((), ()))
NN = (((1,), (0,)), ((), ()))
OFFS = (0, -1, 1, 2)

SMEM = pl.BlockSpec(memory_space=pltpu.SMEM)
VMEM = pl.BlockSpec(memory_space=pltpu.VMEM)


def mm(a, b, dims=NN):
    return lax.dot_general(a, b, dims, preferred_element_type=F32)


def iota(shape, axis):
    return lax.broadcasted_iota(I32, shape, axis)


def onehot(mask):
    return jnp.where(mask, F32(1.0), F32(0.0))


COST = {
    "pack": 2, "send": 3, "weight_send": 4, "weight_join": 6, "gate_up": 7, "back": 5, "mid": 10,
    "wgrad_other": 8, "wgrad_own": 8, "finish": 2, "collect": 3, "merge": 2, "assemble": 2,
}


def call(body, outs, args, scratch=(), name=None):
    return pl.pallas_call(
        body,
        out_shape=[jax.ShapeDtypeStruct(s, t) for s, t in outs],
        in_specs=[SMEM] + [VMEM] * (len(args) - 1),
        out_specs=[VMEM] * len(outs),
        scratch_shapes=list(scratch),
        compiler_params=pltpu.CompilerParams(vmem_limit_bytes=60 * 1024 * 1024),
        cost_estimate=pl.CostEstimate(
            flops=COST[name] * 100_000_000_000, transcendentals=0, bytes_accessed=0
        ),
        name=name,
    )(*args)


def at(start, size):
    return pl.ds(pl.multiple_of(start, size), size)


def chunk_cols(y, off):
    return at(lax.rem(y + (off + 4), 4) * CH, CH)


def row_parts(r):
    e = (r * 2731) >> 16
    q = r - e * GROUP
    core = q >= CAP
    return e, core, jnp.where(core, q - CAP, q)


def slot_key(ids):
    e = iota((EXPERTS, 128), 0)
    member = jnp.zeros((EXPERTS, 128), F32)
    for k in range(TOP):
        member = member + onehot(ids[k : k + 1, :] == e)
    upto = onehot(iota((128, 128), 0) <= iota((128, 128), 1)).astype(BF)
    rank = mm(member.astype(BF), upto) - 1.0
    return jnp.where(member > 0.5, rank, F32(-1.0))


def slot_weight(ids, comb):
    e = iota((EXPERTS, 128), 0)
    out = jnp.zeros((EXPERTS, 128), F32)
    for k in range(TOP):
        out = out + jnp.where(ids[k : k + 1, :] == e, comb[k : k + 1, :], F32(0.0))
    return out.astype(BF)


def expert_rows():
    e, _, _ = row_parts(iota((ROWS, EXPERTS), 0))
    return onehot(e == iota((ROWS, EXPERTS), 1)).astype(BF)


def got_ids(pk):
    return pk[256:272, :128].astype(F32)[:8].astype(I32)


def pack_body(pos, ids, comb, tokens, grads, out):
    cols = at((1 - pos[1]) * HALF + pos[0] * CH, CH)
    out[:128, :] = tokens[:, cols]
    out[128:256, :] = grads[:, cols]
    row = jnp.concatenate(
        [ids[...].astype(F32), comb[...].astype(F32), jnp.zeros((8, 256), F32)], axis=1
    )
    out[256:, :] = jnp.concatenate([row, jnp.zeros((8, CH), F32)], axis=0).astype(BF)


def send_body(weighted, pos, ids, comb, pk, rows_ref, out):
    y, h = pos[0], pos[1]
    rows = expert_rows()
    _, core, slot = row_parts(iota((ROWS, 128), 0))
    slot = slot.astype(F32)
    parts = []
    for mine, idv, cv in (
        (True, ids[...], comb[...].astype(F32)),
        (False, got_ids(pk), pk[256:272, 128:256].astype(F32)[:8]),
    ):
        key = mm(rows, slot_key(idv).astype(BF))
        member = (key == slot) & (core == ((h == 1) if mine else (h == 0)))
        if weighted:
            parts.append(jnp.where(member, mm(rows, slot_weight(idv, cv)), F32(0.0)))
        else:
            parts.append(onehot(member))
    lhs = jnp.concatenate(parts, axis=1).astype(BF)
    got = pk[128:256, :] if weighted else pk[:128, :]
    rhs = jnp.concatenate([rows_ref[:, at(h * HALF + y * CH, CH)], got], axis=0)
    out[...] = mm(lhs, rhs).astype(BF)


def weight_send_body(pos, gw, uw, dw, out):
    other = at((1 - pos[1]) * HALF, HALF)
    for m, w in enumerate((gw, uw, dw)):
        out[m] = w[:, other]


def weight_join_body(pos, gw, uw, dw, got, out):
    h = pos[1]
    for m, w in enumerate((gw, uw, dw)):
        out[m, at(h * 192, 192), :] = w[:, at(h * HALF, HALF)]
        out[m, at((1 - h) * 192, 192), :] = got[m]


def partial_body(first, count, pos, x0, x1, x2, x3, w, out):
    y = pos[0]

    def block(i, carry):
        rs = at(i * 256, 256)
        acc = None
        for x, off in zip((x0, x1, x2, x3), OFFS):
            wc = w[first : first + count, :, chunk_cols(y, off)].reshape(count * UNITS, CH)
            part = mm(x[rs, :], wc, NT)
            acc = part if acc is None else acc + part
        out[rs, :] = acc
        return carry

    lax.fori_loop(0, 3, block, 0)


def input_part(both, w, y, off):
    wc = w[0:2, :, chunk_cols(y, off)].reshape(2 * UNITS, CH)
    return (mm(both[...], wc) * (2 * FF) ** (-0.5)).astype(BF)


def mid_body(pos, gu_a, gu_b, bk_a, bk_b, w, both, hd, cb, d2, dp, dm, d0):
    y, h = pos[0], pos[1]
    scale = D**-0.5
    own = (iota((128, UNITS), 1) >= 192) == (h == 1)

    def block(i, carry):
        rs = at(i * 128, 128)
        gate = (gu_a[rs, :UNITS] + gu_b[rs, :UNITS]) * scale
        up = (gu_a[rs, UNITS:] + gu_b[rs, UNITS:]) * scale
        back = bk_a[rs, :] + bk_b[rs, :]
        sig = jax.nn.sigmoid(gate)
        active = gate * sig
        hidden = active * up
        slope = sig * (1.0 + gate * (1.0 - sig))
        scaled = back * scale
        both[rs, :UNITS] = (scaled * up * slope).astype(BF)
        both[rs, UNITS:] = (scaled * active).astype(BF)
        hd[rs, :] = hidden.astype(BF)
        c = jnp.sum(jnp.where(own, hidden * back, F32(0.0)), axis=1, keepdims=True)
        cb[rs, :] = jnp.broadcast_to(c * (D * FF) ** (-0.5), (128, 128)).astype(BF)
        return carry

    lax.fori_loop(0, 6, block, 0)
    d2[...] = input_part(both, w, y, 2)
    dp[...] = input_part(both, w, y, 1)
    dm[...] = input_part(both, w, y, -1)
    d0[...] = input_part(both, w, y, 0)


def finish_body(pos, d0, a, b, c, out):
    total = d0[...].astype(F32) + a[...].astype(F32) + b[...].astype(F32) + c[...].astype(F32)
    out[...] = total.astype(BF)


def wgrad(pos, half, gu_t, hd_t, xs, gs, store):
    y = pos[0]
    rows = at(half * 192, 192)
    lhs = gu_t[:, rows, :].reshape(2 * 192, ROWS)
    low = hd_t[rows, :]
    factor = 512.0 ** (-0.5)
    for x, g, off in zip(xs, gs, OFFS):
        part = (mm(lhs, x[...]) * factor).astype(BF)
        c = lax.rem(y + (off + 4), 4) * CH
        store(0, c, part[:192])
        store(1, c, part[192:])
        store(2, c, (mm(low, g[...]) * factor).astype(BF))


def wgrad_other_body(pos, both, hd, *refs):
    xs, gs, (gu_t, hd_t, out) = refs[:4], refs[4:8], refs[8:]
    for m in range(2):
        gu_t[m] = both[:, m * UNITS : (m + 1) * UNITS].T
    hd_t[...] = hd[...].T

    def store(m, c, part):
        out[m, :, at(c, CH)] = part

    wgrad(pos, 1 - pos[1], gu_t, hd_t, xs, gs, store)


def wgrad_own_body(pos, gu_t, hd_t, got, *refs):
    xs, gs, outs = refs[:4], refs[4:8], refs[8:]
    h = pos[1]
    for m in range(3):
        outs[m][:, at((1 - h) * HALF, HALF)] = got[m]

    def store(m, c, part):
        outs[m][:, at(h * HALF + c, CH)] = part

    wgrad(pos, h, gu_t, hd_t, xs, gs, store)


def hi_lo(x):
    hi = x.astype(BF).astype(F32)
    wide = jnp.concatenate([hi, x - hi], axis=0)
    return jnp.concatenate([wide, jnp.zeros((16, CH - 128), F32)], axis=1).astype(BF)


def collect_body(pos, ids, pk, r, cb, q, cg, sib):
    h = pos[1]
    pair = (ids[...], got_ids(pk))
    key = jnp.concatenate([slot_key(i).T for i in pair], axis=0).astype(BF)
    rows = expert_rows()
    key = mm(key, rows, NT)
    _, core, slot = row_parts(iota((256, ROWS), 1))
    core = core == ((iota((256, ROWS), 0) >= 128) != (h == 1))
    lhs = onehot((key == slot.astype(F32)) & core).astype(BF)
    acc = mm(lhs, r[...])
    q[...] = acc[:128].astype(BF)
    sib[:128, :] = acc[128:].astype(BF)
    tokw = mm(lhs, (cb[:, :EXPERTS].astype(F32) * rows.astype(F32)).astype(BF))
    e = iota((EXPERTS, 128), 0)
    sums = []
    for b, idv in enumerate(pair):
        tw = tokw[b * 128 : (b + 1) * 128].T
        picked = [
            jnp.sum(jnp.where(idv[k : k + 1, :] == e, tw, F32(0.0)), axis=0, keepdims=True)
            for k in range(TOP)
        ]
        sums.append(jnp.concatenate(picked, axis=0))
    cg[...] = sums[0]
    sib[128:, :] = hi_lo(sums[1])


def merge_body(pos, q, cg, got, out):
    out[:128, :] = q[...]
    out[128:256, :] = got[:128, :]
    tail = got[128:144, :128].astype(F32)
    out[256:, :] = hi_lo(cg[...] + tail[:8] + tail[8:])


def assemble_body(pos, comb, q, left, right, across, out, cg):
    y, h = pos[0], pos[1]
    total = jnp.zeros((16, 128), F32)
    for off, ref in zip(OFFS, (q, left, right, across)):
        c = lax.rem(y + (off + 4), 4) * CH
        out[:, at(h * HALF + c, CH)] = ref[:128, :]
        out[:, at((1 - h) * HALF + c, CH)] = ref[128:256, :]
        total = total + ref[256:272, :128].astype(F32)
    cg[...] = (total[:8] + total[8:]) / comb[...].astype(F32)


def on_device(tokens, out_grad, expert_ids, combine, gate_weight, up_weight, down_weight):
    n_dp = lax.axis_size("dp")
    width = lax.axis_size("expert")
    up_ring = [(i, (i + 1) % n_dp) for i in range(n_dp)]
    down_ring = [(i, (i - 1) % n_dp) for i in range(n_dp)]
    far = [(i, (i + 2) % n_dp) for i in range(n_dp)]
    cores = [(i, i ^ 1) for i in range(width)]
    same_core = [list(range(c, width, 2)) for c in range(2)]

    def up(x):
        return lax.ppermute(x, "dp", up_ring)

    def down(x):
        return lax.ppermute(x, "dp", down_ring)

    def swap(x):
        return lax.ppermute(x, "expert", cores)

    def exchange(x):
        n = x.shape[1]
        x = x.reshape(EXPERTS, GROUP, n)
        x = lax.all_to_all(
            x, "expert", split_axis=0, concat_axis=0, axis_index_groups=same_core, tiled=True
        )
        return x.reshape(ROWS, n)

    def across(x):
        return lax.ppermute(x, "dp", far)

    def spread(x):
        return x, up(x), down(x), across(x)

    tie = lax.optimization_barrier
    pos = jnp.stack([lax.axis_index("dp"), lax.axis_index("expert") & 1]).astype(I32)
    ids = expert_ids.T
    comb = combine.T
    gw, uw, dw = gate_weight[0], up_weight[0], down_weight[0]

    (pk,) = call(
        pack_body, [((272, CH), BF)], (pos, ids, comb, tokens, out_grad), name="pack"
    )
    pk = swap(pk)

    def send(weighted, rows):
        return call(
            functools.partial(send_body, weighted), [((ROWS, CH), BF)],
            (pos, ids, comb, pk, rows), name="send",
        )[0]

    xs = exchange(send(False, tokens))
    gs, xs = tie((send(True, out_grad), xs))
    gs = exchange(gs)
    (wsend,) = call(
        weight_send_body, [((3, 192, HALF), BF)], (pos, gw, uw, dw), name="weight_send"
    )
    wgot = swap(wsend)
    (wall,) = call(
        weight_join_body, [((3, UNITS, HALF), BF)], (pos, gw, uw, dw, wgot), name="weight_join"
    )
    xs, gs = spread(xs), spread(gs)
    (gu_a,) = call(
        functools.partial(partial_body, 0, 2), [((ROWS, 2 * UNITS), F32)], (pos, *xs, wall),
        name="gate_up",
    )
    gu_b = swap(gu_a)
    (bk_a,) = call(
        functools.partial(partial_body, 2, 1), [((ROWS, UNITS), F32)], (pos, *gs, wall),
        name="back",
    )
    bk_b = swap(bk_a)
    both, hd, cb, d2, dp, dm, d0 = call(
        mid_body,
        [((ROWS, 2 * UNITS), BF), ((ROWS, UNITS), BF), ((ROWS, 128), BF)]
        + [((ROWS, CH), BF)] * 4,
        (pos, gu_a, gu_b, bk_a, bk_b, wall), name="mid",
    )
    d2, dp, dm = across(d2), up(dp), down(dm)
    dp, cb = tie((dp, cb))
    cb = exchange(cb)
    gu_t, hd_t, dsend = call(
        wgrad_other_body,
        [((2, UNITS, ROWS), BF), ((UNITS, ROWS), BF), ((3, 192, HALF), BF)],
        (pos, both, hd, *xs, *gs), name="wgrad_other",
    )
    dgot = swap(dsend)
    d0, gu_t, cb = tie((d0, gu_t, cb))
    (r,) = call(finish_body, [((ROWS, CH), BF)], (pos, d0, dp, dm, d2), name="finish")
    gu_t, r = tie((gu_t, r))
    r = exchange(r)
    dwg, dwu, dwd = call(
        wgrad_own_body, [((192, D), BF)] * 3, (pos, gu_t, hd_t, dgot, *xs, *gs),
        name="wgrad_own",
    )
    r, dwg = tie((r, dwg))
    q, cg, sib = call(
        collect_body, [((128, CH), BF), ((TOP, 128), F32), ((144, CH), BF)],
        (pos, ids, pk, r, cb), name="collect",
    )
    got = swap(sib)
    (q,) = call(merge_body, [((272, CH), BF)], (pos, q, cg, got), name="merge")
    input_grad, cg = call(
        assemble_body, [((128, D), BF), ((TOP, 128), F32)], (pos, comb, *spread(q)),
        name="assemble",
    )
    return (input_grad, cg.T, dwg[None], dwu[None], dwd[None])


def solution(mesh):
    rows = P("expert", None)
    units = P("expert", "dp", None)
    return jax.shard_map(
        on_device,
        mesh=mesh,
        in_specs=(rows, rows, rows, rows, units, units, units),
        out_specs=(rows, rows, units, units, units),
        check_vma=False,
    )
```

```python
import functools

import jax
import jax.numpy as jnp
from jax import lax
from jax.experimental import pallas as pl
from jax.experimental.pallas import tpu as pltpu
from jax.sharding import PartitionSpec as P

D = 4096
FF = 1536
TOP = 8
EXPERTS = 32
BF = jnp.bfloat16
F32 = jnp.float32
I32 = jnp.int32
HALF = D // 2
CH = 512
CAP = 12
GROUP = 2 * CAP
ROWS = EXPERTS * GROUP
UNITS = 384
NT = (((1,), (1,)), ((), ()))
NN = (((1,), (0,)), ((), ()))
HR = ROWS // 2
OFFS = (0, -1, 1, 2)

SMEM = pl.BlockSpec(memory_space=pltpu.SMEM)
VMEM = pl.BlockSpec(memory_space=pltpu.VMEM)


def mm(a, b, dims=NN):
    return lax.dot_general(a, b, dims, preferred_element_type=F32)


def iota(shape, axis):
    return lax.broadcasted_iota(I32, shape, axis)


def onehot(mask):
    return jnp.where(mask, F32(1.0), F32(0.0))


COST = {
    "pack": 2, "send": 3, "weight_send": 4, "weight_join": 6, "gate_up": 8, "back_near": 5, "back": 3,
    "mid": 8, "rest": 4, "pass_on": 2,
    "wgrad": 13, "wgrad_join": 5, "finish": 2, "collect": 3, "merge": 2, "assemble": 2,
}


def call(body, outs, args, scratch=(), name=None):
    return pl.pallas_call(
        body,
        out_shape=[jax.ShapeDtypeStruct(s, t) for s, t in outs],
        in_specs=[SMEM] + [VMEM] * (len(args) - 1),
        out_specs=[VMEM] * len(outs),
        scratch_shapes=list(scratch),
        compiler_params=pltpu.CompilerParams(vmem_limit_bytes=60 * 1024 * 1024),
        cost_estimate=pl.CostEstimate(
            flops=COST[name] * 100_000_000_000, transcendentals=0, bytes_accessed=0
        ),
        name=name,
    )(*args)


def at(start, size):
    return pl.ds(pl.multiple_of(start, size), size)


def chunk_cols(y, off):
    return at(lax.rem(y + (off + 4), 4) * CH, CH)


def row_parts(r):
    e = (r * 2731) >> 16
    q = r - e * GROUP
    core = q >= CAP
    return e, core, jnp.where(core, q - CAP, q)


def slot_key(ids):
    e = iota((EXPERTS, 128), 0)
    member = jnp.zeros((EXPERTS, 128), F32)
    for k in range(TOP):
        member = member + onehot(ids[k : k + 1, :] == e)
    upto = onehot(iota((128, 128), 0) <= iota((128, 128), 1)).astype(BF)
    rank = mm(member.astype(BF), upto) - 1.0
    return jnp.where(member > 0.5, rank, F32(-1.0))


def slot_weight(ids, comb):
    e = iota((EXPERTS, 128), 0)
    out = jnp.zeros((EXPERTS, 128), F32)
    for k in range(TOP):
        out = out + jnp.where(ids[k : k + 1, :] == e, comb[k : k + 1, :], F32(0.0))
    return out.astype(BF)


def expert_rows():
    e, _, _ = row_parts(iota((ROWS, EXPERTS), 0))
    return onehot(e == iota((ROWS, EXPERTS), 1)).astype(BF)


def got_ids(pk):
    return pk[256:272, :128].astype(F32)[:8].astype(I32)


def pack_body(pos, ids, comb, tokens, grads, out):
    cols = at((1 - pos[1]) * HALF + pos[0] * CH, CH)
    out[:128, :] = tokens[:, cols]
    out[128:256, :] = grads[:, cols]
    row = jnp.concatenate(
        [ids[...].astype(F32), comb[...].astype(F32), jnp.zeros((8, 256), F32)], axis=1
    )
    out[256:, :] = jnp.concatenate([row, jnp.zeros((8, CH), F32)], axis=0).astype(BF)


def send_body(weighted, pos, ids, comb, pk, rows_ref, out):
    y, h = pos[0], pos[1]
    rows = expert_rows()
    _, core, slot = row_parts(iota((ROWS, 128), 0))
    slot = slot.astype(F32)
    parts = []
    for mine, idv, cv in (
        (True, ids[...], comb[...].astype(F32)),
        (False, got_ids(pk), pk[256:272, 128:256].astype(F32)[:8]),
    ):
        key = mm(rows, slot_key(idv).astype(BF))
        member = (key == slot) & (core == ((h == 1) if mine else (h == 0)))
        if weighted:
            parts.append(jnp.where(member, mm(rows, slot_weight(idv, cv)), F32(0.0)))
        else:
            parts.append(onehot(member))
    lhs = jnp.concatenate(parts, axis=1).astype(BF)
    got = pk[128:256, :] if weighted else pk[:128, :]
    rhs = jnp.concatenate([rows_ref[:, at(h * HALF + y * CH, CH)], got], axis=0)
    out[...] = mm(lhs, rhs).astype(BF)


def weight_send_body(pos, gw, uw, dw, out):
    other = at((1 - pos[1]) * HALF, HALF)
    for m, w in enumerate((gw, uw, dw)):
        out[m] = w[:, other]


def weight_join_body(pos, gw, uw, dw, got, out):
    h = pos[1]
    for m, w in enumerate((gw, uw, dw)):
        out[m, at(h * 192, 192), :] = w[:, at(h * HALF, HALF)]
        out[m, at((1 - h) * 192, 192), :] = got[m]


def unit_weights(w, first, count, y, off):
    return w[first : first + count, :, chunk_cols(y, off)].reshape(count * UNITS, CH)


def near(first, count, y, xs, w, out):
    def block(i, carry):
        rs = at(i * 256, 256)
        acc = None
        for x, off in zip(xs, OFFS[:3]):
            part = mm(x[rs, :], unit_weights(w, first, count, y, off), NT)
            acc = part if acc is None else acc + part
        out[rs, :] = acc
        return carry

    lax.fori_loop(0, 3, block, 0)


def gate_up_body(pos, x0, x1, x2, xa, xb, w, out):
    y = pos[0]
    near(0, 2, y, (x0, x1, x2), w, out)
    wc = unit_weights(w, 0, 2, y, 2)
    out[:HR, :] += mm(xa[...], wc, NT)
    out[HR:, :] += mm(xb[...], wc, NT)


def back_near_body(pos, x0, x1, x2, w, out):
    near(2, 1, pos[0], (x0, x1, x2), w, out)


def back_body(pos, acc, xa, xb, w, out):
    wc = unit_weights(w, 2, 1, pos[0], 2)
    out[:HR, :] = acc[:HR, :] + mm(xa[...], wc, NT)
    out[HR:, :] = acc[HR:, :] + mm(xb[...], wc, NT)


def input_part(both, w, y, off):
    wc = unit_weights(w, 0, 2, y, off)
    return (mm(both[...], wc) * (2 * FF) ** (-0.5)).astype(BF)


def mid_body(pos, gu_a, gu_b, bk_a, bk_b, w, both, hd, cb, d2a, d2b):
    y, h = pos[0], pos[1]
    scale = D**-0.5
    own = (iota((128, UNITS), 1) >= 192) == (h == 1)

    def block(i, carry):
        rs = at(i * 128, 128)
        gate = (gu_a[rs, :UNITS] + gu_b[rs, :UNITS]) * scale
        up = (gu_a[rs, UNITS:] + gu_b[rs, UNITS:]) * scale
        back = bk_a[rs, :] + bk_b[rs, :]
        sig = jax.nn.sigmoid(gate)
        active = gate * sig
        hidden = active * up
        slope = sig * (1.0 + gate * (1.0 - sig))
        scaled = back * scale
        both[rs, :UNITS] = (scaled * up * slope).astype(BF)
        both[rs, UNITS:] = (scaled * active).astype(BF)
        hd[rs, :] = hidden.astype(BF)
        c = jnp.sum(jnp.where(own, hidden * back, F32(0.0)), axis=1, keepdims=True)
        cb[rs, :] = jnp.broadcast_to(c * (D * FF) ** (-0.5), (128, 128)).astype(BF)
        return carry

    lax.fori_loop(0, 6, block, 0)
    part = input_part(both, w, y, 2)
    d2a[...] = part[:HR]
    d2b[...] = part[HR:]


def rest_body(pos, both, w, dpa, dpb, dma, dmb, d0):
    y = pos[0]
    for off, (top, bottom) in ((1, (dpa, dpb)), (-1, (dma, dmb))):
        part = input_part(both, w, y, off)
        top[...] = part[:HR]
        bottom[...] = part[HR:]
    d0[...] = input_part(both, w, y, 0)


def pass_on_body(pos, dpa, r2, dmb, q2, pa, mb):
    pa[...] = (dpa[...].astype(F32) + r2[...].astype(F32)).astype(BF)
    mb[...] = (dmb[...].astype(F32) + q2[...].astype(F32)).astype(BF)


def finish_body(pos, d0, ma, pa, mb, pb, out):
    for rs, a, b in ((slice(0, HR), ma, pa), (slice(HR, ROWS), mb, pb)):
        total = d0[rs, :].astype(F32) + a[...].astype(F32) + b[...].astype(F32)
        out[rs, :] = total.astype(BF)


def wgrad(pos, half, gu_t, hd_t, xs, gs, store):
    y = pos[0]
    rows = at(half * 192, 192)
    lhs = gu_t[:, rows, :].reshape(2 * 192, ROWS)
    low = hd_t[rows, :]
    factor = 512.0 ** (-0.5)
    for i, off in enumerate(OFFS):
        if i < 3:
            part, last = mm(lhs, xs[i][...]), mm(low, gs[i][...])
        else:
            part = mm(lhs[:, :HR], xs[3][...]) + mm(lhs[:, HR:], xs[4][...])
            last = mm(low[:, :HR], gs[3][...]) + mm(low[:, HR:], gs[4][...])
        part = (part * factor).astype(BF)
        c = lax.rem(y + (off + 4), 4) * CH
        store(0, c, part[:192])
        store(1, c, part[192:])
        store(2, c, (last * factor).astype(BF))


def wgrad_body(pos, both, hd, *refs):
    xs, gs, (own, other, gu_t, hd_t) = refs[:5], refs[5:10], refs[10:]
    h = pos[1]
    for m in range(2):
        gu_t[m] = both[:, m * UNITS : (m + 1) * UNITS].T
    hd_t[...] = hd[...].T
    for half, out in ((1 - h, other), (h, own)):

        def store(m, c, part, out=out):
            out[m, :, at(c, CH)] = part

        wgrad(pos, half, gu_t, hd_t, xs, gs, store)


def wgrad_join_body(pos, own, got, *outs):
    h = pos[1]
    for m in range(3):
        outs[m][:, at(h * HALF, HALF)] = own[m]
        outs[m][:, at((1 - h) * HALF, HALF)] = got[m]


def hi_lo(x):
    hi = x.astype(BF).astype(F32)
    wide = jnp.concatenate([hi, x - hi], axis=0)
    return jnp.concatenate([wide, jnp.zeros((16, CH - 128), F32)], axis=1).astype(BF)


def collect_body(pos, ids, pk, r, cb, q, cg, sib):
    h = pos[1]
    pair = (ids[...], got_ids(pk))
    key = jnp.concatenate([slot_key(i).T for i in pair], axis=0).astype(BF)
    rows = expert_rows()
    key = mm(key, rows, NT)
    _, core, slot = row_parts(iota((256, ROWS), 1))
    core = core == ((iota((256, ROWS), 0) >= 128) != (h == 1))
    lhs = onehot((key == slot.astype(F32)) & core).astype(BF)
    acc = mm(lhs, r[...])
    q[...] = acc[:128].astype(BF)
    sib[:128, :] = acc[128:].astype(BF)
    tokw = mm(lhs, (cb[:, :EXPERTS].astype(F32) * rows.astype(F32)).astype(BF))
    e = iota((EXPERTS, 128), 0)
    sums = []
    for b, idv in enumerate(pair):
        tw = tokw[b * 128 : (b + 1) * 128].T
        picked = [
            jnp.sum(jnp.where(idv[k : k + 1, :] == e, tw, F32(0.0)), axis=0, keepdims=True)
            for k in range(TOP)
        ]
        sums.append(jnp.concatenate(picked, axis=0))
    cg[...] = sums[0]
    sib[128:, :] = hi_lo(sums[1])


def merge_body(pos, q, cg, got, out):
    out[:128, :] = q[...]
    out[128:256, :] = got[:128, :]
    tail = got[128:144, :128].astype(F32)
    out[256:, :] = hi_lo(cg[...] + tail[:8] + tail[8:])


def assemble_body(pos, comb, q, left, right, across, out, cg):
    y, h = pos[0], pos[1]
    total = jnp.zeros((16, 128), F32)
    for off, ref in zip(OFFS, (q, left, right, across)):
        c = lax.rem(y + (off + 4), 4) * CH
        out[:, at(h * HALF + c, CH)] = ref[:128, :]
        out[:, at((1 - h) * HALF + c, CH)] = ref[128:256, :]
        total = total + ref[256:272, :128].astype(F32)
    cg[...] = (total[:8] + total[8:]) / comb[...].astype(F32)


def on_device(tokens, out_grad, expert_ids, combine, gate_weight, up_weight, down_weight):
    n_dp = lax.axis_size("dp")
    width = lax.axis_size("expert")
    up_ring = [(i, (i + 1) % n_dp) for i in range(n_dp)]
    down_ring = [(i, (i - 1) % n_dp) for i in range(n_dp)]
    far = [(i, (i + 2) % n_dp) for i in range(n_dp)]
    cores = [(i, i ^ 1) for i in range(width)]
    same_core = [list(range(c, width, 2)) for c in range(2)]

    def up(x):
        return lax.ppermute(x, "dp", up_ring)

    def down(x):
        return lax.ppermute(x, "dp", down_ring)

    def swap(x):
        return lax.ppermute(x, "expert", cores)

    def exchange(x):
        n = x.shape[1]
        x = x.reshape(EXPERTS, GROUP, n)
        x = lax.all_to_all(
            x, "expert", split_axis=0, concat_axis=0, axis_index_groups=same_core, tiled=True
        )
        return x.reshape(ROWS, n)

    def across(x):
        return lax.ppermute(x, "dp", far)

    def spread(x):
        left, right = up(x), down(x)
        return x, left, right, up(left[:HR]), down(right[HR:])

    tie = lax.optimization_barrier
    pos = jnp.stack([lax.axis_index("dp"), lax.axis_index("expert") & 1]).astype(I32)
    ids = expert_ids.T
    comb = combine.T
    gw, uw, dw = gate_weight[0], up_weight[0], down_weight[0]

    (pk,) = call(
        pack_body, [((272, CH), BF)], (pos, ids, comb, tokens, out_grad), name="pack"
    )
    pk = swap(pk)

    def send(weighted, rows):
        return call(
            functools.partial(send_body, weighted), [((ROWS, CH), BF)],
            (pos, ids, comb, pk, rows), name="send",
        )[0]

    xs, later = tie((send(False, tokens), pos))
    xs = exchange(xs)
    gs, xs = tie((send(True, out_grad), xs))
    gs = exchange(gs)
    (wsend,) = call(
        weight_send_body, [((3, 192, HALF), BF)], (later, gw, uw, dw), name="weight_send"
    )
    wgot = swap(wsend)
    (wall,) = call(
        weight_join_body, [((3, UNITS, HALF), BF)], (pos, gw, uw, dw, wgot), name="weight_join"
    )
    xs, gs = spread(xs), spread(gs)
    (gu_a,) = call(gate_up_body, [((ROWS, 2 * UNITS), F32)], (pos, *xs, wall), name="gate_up")
    gu_b = swap(gu_a)
    (bk_a,) = call(
        back_near_body, [((ROWS, UNITS), F32)], (pos, *gs[:3], wall), name="back_near"
    )
    (bk_a,) = call(
        back_body, [((ROWS, UNITS), F32)], (pos, bk_a, *gs[3:], wall), name="back"
    )
    bk_b = swap(bk_a)
    both, hd, cb, d2a, d2b = call(
        mid_body,
        [((ROWS, 2 * UNITS), BF), ((ROWS, UNITS), BF), ((ROWS, 128), BF)]
        + [((HR, CH), BF)] * 2,
        (pos, gu_a, gu_b, bk_a, bk_b, wall), name="mid",
    )
    r2, q2 = up(d2a), down(d2b)
    dpa, dpb, dma, dmb, d0 = call(
        rest_body, [((HR, CH), BF)] * 4 + [((ROWS, CH), BF)], (pos, both, wall), name="rest"
    )
    pb, ma = up(dpb), down(dma)
    pa, mb = call(pass_on_body, [((HR, CH), BF)] * 2, (pos, dpa, r2, dmb, q2), name="pass_on")
    pa, mb = up(pa), down(mb)
    pb, cb = tie((pb, cb))
    cb = exchange(cb)
    d0, cb = tie((d0, cb))
    (r,) = call(finish_body, [((ROWS, CH), BF)], (pos, d0, ma, pa, mb, pb), name="finish")
    both, r = tie((both, r))
    r = exchange(r)
    w_own, w_other = call(
        wgrad_body, [((3, 192, HALF), BF)] * 2, (pos, both, hd, *xs, *gs),
        scratch=[pltpu.VMEM((2, UNITS, ROWS), BF), pltpu.VMEM((UNITS, ROWS), BF)],
        name="wgrad",
    )
    r, w_other = tie((r, w_other))
    dgot = swap(w_other)
    q, cg, sib = call(
        collect_body, [((128, CH), BF), ((TOP, 128), F32), ((144, CH), BF)],
        (pos, ids, pk, r, cb), name="collect",
    )
    got = swap(sib)
    (q,) = call(merge_body, [((272, CH), BF)], (pos, q, cg, got), name="merge")
    q, w_own = tie((q, w_own))
    dwg, dwu, dwd = call(
        wgrad_join_body, [((192, D), BF)] * 3, (pos, w_own, dgot), name="wgrad_join"
    )
    comb, dwg = tie((comb, dwg))
    input_grad, cg = call(
        assemble_body, [((128, D), BF), ((TOP, 128), F32)], (pos, comb, q, up(q), down(q), across(q)),
        name="assemble",
    )
    return (input_grad, cg.T, dwg[None], dwu[None], dwd[None])


def solution(mesh):
    rows = P("expert", None)
    units = P("expert", "dp", None)
    return jax.shard_map(
        on_device,
        mesh=mesh,
        in_specs=(rows, rows, rows, rows, units, units, units),
        out_specs=(rows, rows, units, units, units),
        check_vma=False,
    )
```

```python
import functools

import jax
import jax.numpy as jnp
from jax import lax
from jax.experimental import pallas as pl
from jax.experimental.pallas import tpu as pltpu
from jax.sharding import PartitionSpec as P

D = 4096
FF = 1536
TOP = 8
EXPERTS = 32
BF = jnp.bfloat16
F32 = jnp.float32
I32 = jnp.int32
HALF = D // 2
CH = 512
CAP = 12
GROUP = 2 * CAP
ROWS = EXPERTS * GROUP
UNITS = 384
NT = (((1,), (1,)), ((), ()))
NN = (((1,), (0,)), ((), ()))
HR = ROWS // 2
OFFS = (0, -1, 1, 2)

SMEM = pl.BlockSpec(memory_space=pltpu.SMEM)
VMEM = pl.BlockSpec(memory_space=pltpu.VMEM)


def mm(a, b, dims=NN):
    return lax.dot_general(a, b, dims, preferred_element_type=F32)


def iota(shape, axis):
    return lax.broadcasted_iota(I32, shape, axis)


def onehot(mask):
    return jnp.where(mask, F32(1.0), F32(0.0))


COST = {
    "pack": 2, "send": 3, "weight_send": 4, "weight_join": 6, "gate_up": 8, "back_near": 5, "back": 3,
    "mid": 8, "rest": 4, "pass_on": 2,
    "wgrad": 13, "wgrad_join": 5, "finish": 2, "collect": 3, "assemble": 2,
}


def call(body, outs, args, scratch=(), name=None):
    return pl.pallas_call(
        body,
        out_shape=[jax.ShapeDtypeStruct(s, t) for s, t in outs],
        in_specs=[SMEM] + [VMEM] * (len(args) - 1),
        out_specs=[VMEM] * len(outs),
        scratch_shapes=list(scratch),
        compiler_params=pltpu.CompilerParams(vmem_limit_bytes=60 * 1024 * 1024),
        cost_estimate=pl.CostEstimate(
            flops=COST[name] * 100_000_000_000, transcendentals=0, bytes_accessed=0
        ),
        name=name,
    )(*args)


def at(start, size):
    return pl.ds(pl.multiple_of(start, size), size)


def chunk_cols(y, off):
    return at(lax.rem(y + (off + 4), 4) * CH, CH)


def row_parts(r):
    e = (r * 2731) >> 16
    q = r - e * GROUP
    core = q >= CAP
    return e, core, jnp.where(core, q - CAP, q)


def slot_key(ids):
    e = iota((EXPERTS, 128), 0)
    member = jnp.zeros((EXPERTS, 128), F32)
    for k in range(TOP):
        member = member + onehot(ids[k : k + 1, :] == e)
    upto = onehot(iota((128, 128), 0) <= iota((128, 128), 1)).astype(BF)
    rank = mm(member.astype(BF), upto) - 1.0
    return jnp.where(member > 0.5, rank, F32(-1.0))


def slot_weight(ids, comb):
    e = iota((EXPERTS, 128), 0)
    out = jnp.zeros((EXPERTS, 128), F32)
    for k in range(TOP):
        out = out + jnp.where(ids[k : k + 1, :] == e, comb[k : k + 1, :], F32(0.0))
    return out.astype(BF)


def expert_rows():
    e, _, _ = row_parts(iota((ROWS, EXPERTS), 0))
    return onehot(e == iota((ROWS, EXPERTS), 1)).astype(BF)


def got_ids(pk):
    return pk[256:272, :128].astype(F32)[:8].astype(I32)


def pack_body(pos, ids, comb, tokens, grads, out):
    cols = at((1 - pos[1]) * HALF + pos[0] * CH, CH)
    out[:128, :] = tokens[:, cols]
    out[128:256, :] = grads[:, cols]
    row = jnp.concatenate(
        [ids[...].astype(F32), comb[...].astype(F32), jnp.zeros((8, 256), F32)], axis=1
    )
    out[256:, :] = jnp.concatenate([row, jnp.zeros((8, CH), F32)], axis=0).astype(BF)


def send_body(weighted, pos, ids, comb, pk, rows_ref, out):
    y, h = pos[0], pos[1]
    rows = expert_rows()
    _, core, slot = row_parts(iota((ROWS, 128), 0))
    slot = slot.astype(F32)
    parts = []
    for mine, idv, cv in (
        (True, ids[...], comb[...].astype(F32)),
        (False, got_ids(pk), pk[256:272, 128:256].astype(F32)[:8]),
    ):
        key = mm(rows, slot_key(idv).astype(BF))
        member = (key == slot) & (core == ((h == 1) if mine else (h == 0)))
        if weighted:
            parts.append(jnp.where(member, mm(rows, slot_weight(idv, cv)), F32(0.0)))
        else:
            parts.append(onehot(member))
    lhs = jnp.concatenate(parts, axis=1).astype(BF)
    got = pk[128:256, :] if weighted else pk[:128, :]
    rhs = jnp.concatenate([rows_ref[:, at(h * HALF + y * CH, CH)], got], axis=0)
    out[...] = mm(lhs, rhs).astype(BF)


def weight_send_body(pos, gw, uw, dw, out):
    other = at((1 - pos[1]) * HALF, HALF)
    for m, w in enumerate((gw, uw, dw)):
        out[m] = w[:, other]


def weight_join_body(pos, gw, uw, dw, got, gu, down):
    h = pos[1]
    for m, w in enumerate((gw, uw)):
        gu[m, at(h * 192, 192), :] = w[:, at(h * HALF, HALF)]
        gu[m, at((1 - h) * 192, 192), :] = got[m]
    down[at(h * 192, 192), :] = dw[:, at(h * HALF, HALF)]
    down[at((1 - h) * 192, 192), :] = got[2]


def unit_weights(w, y, off):
    return w[:, :, chunk_cols(y, off)].reshape(2 * UNITS, CH)


def gate_up_body(pos, x0, x1, x2, xa, xb, w, out):
    y = pos[0]

    def block(i, carry):
        rs = at(i * 256, 256)
        acc = None
        for x, off in zip((x0, x1, x2), OFFS[:3]):
            part = mm(x[rs, :], unit_weights(w, y, off), NT)
            acc = part if acc is None else acc + part
        out[rs, :] = acc
        return carry

    lax.fori_loop(0, 3, block, 0)
    wc = unit_weights(w, y, 2)
    out[:HR, :] += mm(xa[...], wc, NT)
    out[HR:, :] += mm(xb[...], wc, NT)


def back_near_body(pos, *refs):
    xs, w, out = refs[:6], refs[6], refs[7]
    for half in range(2):
        acc = None
        for x, off in zip(xs[half::2], OFFS[:3]):
            part = mm(x[...], w[:, chunk_cols(pos[0], off)], NT)
            acc = part if acc is None else acc + part
        out[half * HR : (half + 1) * HR, :] = acc


def back_body(pos, acc, xa, xb, w, out):
    wc = w[:, chunk_cols(pos[0], 2)]
    out[:HR, :] = acc[:HR, :] + mm(xa[...], wc, NT)
    out[HR:, :] = acc[HR:, :] + mm(xb[...], wc, NT)


def input_part(both, w, y, off):
    wc = unit_weights(w, y, off)
    return (mm(both[...], wc) * (2 * FF) ** (-0.5)).astype(BF)


def mid_body(pos, gu_a, gu_b, bk_a, bk_b, w, both, hd, cb, d2a, d2b):
    y, h = pos[0], pos[1]
    scale = D**-0.5
    own = (iota((128, UNITS), 1) >= 192) == (h == 1)

    def block(i, carry):
        rs = at(i * 128, 128)
        gate = (gu_a[rs, :UNITS] + gu_b[rs, :UNITS]) * scale
        up = (gu_a[rs, UNITS:] + gu_b[rs, UNITS:]) * scale
        back = bk_a[rs, :] + bk_b[rs, :]
        sig = jax.nn.sigmoid(gate)
        active = gate * sig
        hidden = active * up
        slope = sig * (1.0 + gate * (1.0 - sig))
        scaled = back * scale
        both[rs, :UNITS] = (scaled * up * slope).astype(BF)
        both[rs, UNITS:] = (scaled * active).astype(BF)
        hd[rs, :] = hidden.astype(BF)
        c = jnp.sum(jnp.where(own, hidden * back, F32(0.0)), axis=1, keepdims=True)
        cb[rs, :] = jnp.broadcast_to(c * (D * FF) ** (-0.5), (128, 128)).astype(BF)
        return carry

    lax.fori_loop(0, 6, block, 0)
    part = input_part(both, w, y, 2)
    d2a[...] = part[:HR]
    d2b[...] = part[HR:]


def rest_body(pos, both, w, dpa, dpb, dma, dmb, d0):
    y = pos[0]
    for off, (top, bottom) in ((1, (dpa, dpb)), (-1, (dma, dmb))):
        part = input_part(both, w, y, off)
        top[...] = part[:HR]
        bottom[...] = part[HR:]
    d0[...] = input_part(both, w, y, 0)


def pass_on_body(pos, dpa, r2, dmb, q2, pa, mb):
    pa[...] = (dpa[...].astype(F32) + r2[...].astype(F32)).astype(BF)
    mb[...] = (dmb[...].astype(F32) + q2[...].astype(F32)).astype(BF)


def finish_body(pos, d0, ma, pa, mb, pb, out):
    for rs, a, b in ((slice(0, HR), ma, pa), (slice(HR, ROWS), mb, pb)):
        total = d0[rs, :].astype(F32) + a[...].astype(F32) + b[...].astype(F32)
        out[rs, :] = total.astype(BF)


def wgrad(pos, half, gu_t, hd_t, xs, gs, store):
    y = pos[0]
    rows = at(half * 192, 192)
    lhs = gu_t[:, rows, :].reshape(2 * 192, ROWS)
    low = hd_t[rows, :]
    factor = 512.0 ** (-0.5)
    for i, off in enumerate(OFFS):
        if i < 3:
            part = mm(lhs, xs[i][...])
        else:
            part = mm(lhs[:, :HR], xs[3][...]) + mm(lhs[:, HR:], xs[4][...])
        last = mm(low[:, :HR], gs[2 * i][...]) + mm(low[:, HR:], gs[2 * i + 1][...])
        part = (part * factor).astype(BF)
        c = lax.rem(y + (off + 4), 4) * CH
        store(0, c, part[:192])
        store(1, c, part[192:])
        store(2, c, (last * factor).astype(BF))


def wgrad_body(pos, both, hd, *refs):
    xs, gs, (own, other, gu_t, hd_t) = refs[:5], refs[5:13], refs[13:]
    h = pos[1]
    for m in range(2):
        gu_t[m] = both[:, m * UNITS : (m + 1) * UNITS].T
    hd_t[...] = hd[...].T
    for half, out in ((1 - h, other), (h, own)):

        def store(m, c, part, out=out):
            out[m, :, at(c, CH)] = part

        wgrad(pos, half, gu_t, hd_t, xs, gs, store)


def wgrad_join_body(pos, own, got, *outs):
    h = pos[1]
    for m in range(3):
        outs[m][:, at(h * HALF, HALF)] = own[m]
        outs[m][:, at((1 - h) * HALF, HALF)] = got[m]


def hi_lo(x):
    hi = x.astype(BF).astype(F32)
    wide = jnp.concatenate([hi, x - hi], axis=0)
    return jnp.concatenate([wide, jnp.zeros((16, CH - 128), F32)], axis=1).astype(BF)


def collect_body(pos, ids, pk, r, cb, q, sib):
    h = pos[1]
    pair = (ids[...], got_ids(pk))
    key = jnp.concatenate([slot_key(i).T for i in pair], axis=0).astype(BF)
    rows = expert_rows()
    key = mm(key, rows, NT)
    _, core, slot = row_parts(iota((256, ROWS), 1))
    core = core == ((iota((256, ROWS), 0) >= 128) != (h == 1))
    lhs = onehot((key == slot.astype(F32)) & core).astype(BF)
    acc = mm(lhs, r[...])
    q[:128, :] = acc[:128].astype(BF)
    sib[:128, :] = acc[128:].astype(BF)
    tokw = mm(lhs, (cb[:, :EXPERTS].astype(F32) * rows.astype(F32)).astype(BF))
    e = iota((EXPERTS, 128), 0)
    sums = []
    for b, idv in enumerate(pair):
        tw = tokw[b * 128 : (b + 1) * 128].T
        picked = [
            jnp.sum(jnp.where(idv[k : k + 1, :] == e, tw, F32(0.0)), axis=0, keepdims=True)
            for k in range(TOP)
        ]
        sums.append(jnp.concatenate(picked, axis=0))
    q[128:, :] = hi_lo(sums[0])
    sib[128:, :] = hi_lo(sums[1])


def assemble_body(pos, comb, *refs):
    parts, (out, cg) = refs[:8], refs[8:]
    y, h = pos[0], pos[1]
    total = jnp.zeros((16, 128), F32)
    for i, off in enumerate(OFFS):
        c = lax.rem(y + (off + 4), 4) * CH
        a, b = parts[2 * i], parts[2 * i + 1]
        out[:, at(h * HALF + c, CH)] = a[:128, :]
        out[:, at((1 - h) * HALF + c, CH)] = b[:128, :]
        total = total + a[128:144, :128].astype(F32) + b[128:144, :128].astype(F32)
    cg[...] = (total[:8] + total[8:]) / comb[...].astype(F32)


def on_device(tokens, out_grad, expert_ids, combine, gate_weight, up_weight, down_weight):
    n_dp = lax.axis_size("dp")
    width = lax.axis_size("expert")
    up_ring = [(i, (i + 1) % n_dp) for i in range(n_dp)]
    down_ring = [(i, (i - 1) % n_dp) for i in range(n_dp)]
    cores = [(i, i ^ 1) for i in range(width)]
    same_core = [list(range(c, width, 2)) for c in range(2)]

    def up(x):
        return lax.ppermute(x, "dp", up_ring)

    def down(x):
        return lax.ppermute(x, "dp", down_ring)

    def swap(x):
        return lax.ppermute(x, "expert", cores)

    def exchange(x):
        n = x.shape[1]
        x = x.reshape(EXPERTS, GROUP, n)
        x = lax.all_to_all(
            x, "expert", split_axis=0, concat_axis=0, axis_index_groups=same_core, tiled=True
        )
        return x.reshape(ROWS, n)

    def spread(x):
        left, right = up(x), down(x)
        return x, left, right, up(left[:HR]), down(right[HR:])

    def spread_halves(a, b):
        la, rb, lb, ra = up(a), down(b), up(b), down(a)
        return a, b, la, lb, ra, rb, up(la), down(rb)

    tie = lax.optimization_barrier
    pos = jnp.stack([lax.axis_index("dp"), lax.axis_index("expert") & 1]).astype(I32)
    ids = expert_ids.T
    comb = combine.T
    gw, uw, dw = gate_weight[0], up_weight[0], down_weight[0]

    (pk,) = call(
        pack_body, [((272, CH), BF)], (pos, ids, comb, tokens, out_grad), name="pack"
    )
    pk = swap(pk)

    def send(weighted, rows):
        return call(
            functools.partial(send_body, weighted), [((ROWS, CH), BF)],
            (pos, ids, comb, pk, rows), name="send",
        )[0]

    xs, later = tie((send(False, tokens), pos))
    xs = exchange(xs)
    gs, xs = tie((send(True, out_grad), xs))
    gs = exchange(gs)
    (wsend,) = call(
        weight_send_body, [((3, 192, HALF), BF)], (later, gw, uw, dw), name="weight_send"
    )
    wgot = swap(wsend)
    wgu, wd = call(
        weight_join_body, [((2, UNITS, HALF), BF), ((UNITS, HALF), BF)],
        (pos, gw, uw, dw, wgot), name="weight_join",
    )
    xs, gs = spread(xs), spread_halves(gs[:HR], gs[HR:])
    (gu_a,) = call(gate_up_body, [((ROWS, 2 * UNITS), F32)], (pos, *xs, wgu), name="gate_up")
    gu_b = swap(gu_a)
    (bk_a,) = call(
        back_near_body, [((ROWS, UNITS), F32)], (pos, *gs[:6], wd), name="back_near"
    )
    (bk_a,) = call(
        back_body, [((ROWS, UNITS), F32)], (pos, bk_a, *gs[6:], wd), name="back"
    )
    bk_b = swap(bk_a)
    both, hd, cb, d2a, d2b = call(
        mid_body,
        [((ROWS, 2 * UNITS), BF), ((ROWS, UNITS), BF), ((ROWS, 128), BF)]
        + [((HR, CH), BF)] * 2,
        (pos, gu_a, gu_b, bk_a, bk_b, wgu), name="mid",
    )
    r2, q2 = up(d2a), down(d2b)
    dpa, dpb, dma, dmb, d0 = call(
        rest_body, [((HR, CH), BF)] * 4 + [((ROWS, CH), BF)], (pos, both, wgu), name="rest"
    )
    pb, ma = up(dpb), down(dma)
    pa, mb = call(pass_on_body, [((HR, CH), BF)] * 2, (pos, dpa, r2, dmb, q2), name="pass_on")
    pa, mb = up(pa), down(mb)
    pb, cb = tie((pb, cb))
    cb = exchange(cb)
    (r,) = call(finish_body, [((ROWS, CH), BF)], (pos, d0, ma, pa, mb, pb), name="finish")
    both, r, cb = tie((both, r, cb))
    r = exchange(r)
    w_own, w_other = call(
        wgrad_body, [((3, 192, HALF), BF)] * 2, (pos, both, hd, *xs, *gs),
        scratch=[pltpu.VMEM((2, UNITS, ROWS), BF), pltpu.VMEM((UNITS, ROWS), BF)],
        name="wgrad",
    )
    r, w_other = tie((r, w_other))
    dgot = swap(w_other)
    qa, sib = call(
        collect_body, [((144, CH), BF)] * 2, (pos, ids, pk, r, cb), name="collect"
    )
    qb = swap(sib)
    parts = spread_halves(qa, qb)
    qb, w_own = tie((qb, w_own))
    dwg, dwu, dwd = call(
        wgrad_join_body, [((192, D), BF)] * 3, (pos, w_own, dgot), name="wgrad_join"
    )
    comb, dwg = tie((comb, dwg))
    input_grad, cg = call(
        assemble_body, [((128, D), BF), ((TOP, 128), F32)], (pos, comb, *parts), name="assemble"
    )
    return (input_grad, cg.T, dwg[None], dwu[None], dwd[None])


def solution(mesh):
    rows = P("expert", None)
    units = P("expert", "dp", None)
    return jax.shard_map(
        on_device,
        mesh=mesh,
        in_specs=(rows, rows, rows, rows, units, units, units),
        out_specs=(rows, rows, units, units, units),
        check_vma=False,
    )
```

```python
import functools

import jax
import jax.numpy as jnp
from jax import lax
from jax.experimental import pallas as pl
from jax.experimental.pallas import tpu as pltpu
from jax.sharding import PartitionSpec as P

D = 4096
FF = 1536
TOP = 8
EXPERTS = 32
BF = jnp.bfloat16
F32 = jnp.float32
I32 = jnp.int32
HALF = D // 2
CH = 512
CAP = 12
GROUP = 2 * CAP
ROWS = EXPERTS * GROUP
UNITS = 384
NT = (((1,), (1,)), ((), ()))
NN = (((1,), (0,)), ((), ()))
HR = ROWS // 2
OFFS = (0, -1, 1, 2)

SMEM = pl.BlockSpec(memory_space=pltpu.SMEM)
VMEM = pl.BlockSpec(memory_space=pltpu.VMEM)


def mm(a, b, dims=NN):
    return lax.dot_general(a, b, dims, preferred_element_type=F32)


def iota(shape, axis):
    return lax.broadcasted_iota(I32, shape, axis)


def onehot(mask):
    return jnp.where(mask, F32(1.0), F32(0.0))


COST = {
    "pack": 2, "send": 3, "weight_send": 4, "weight_join": 6, "gate_up": 8, "back_near": 0.02, "back": 3,
    "mid": 8, "rest": 4, "pass_on": 2,
    "wgrad": 6, "wgrad_join": 5, "finish": 2, "collect": 3, "assemble": 2,
}


def call(body, outs, args, scratch=(), name=None):
    return pl.pallas_call(
        body,
        out_shape=[jax.ShapeDtypeStruct(s, t) for s, t in outs],
        in_specs=[SMEM] + [VMEM] * (len(args) - 1),
        out_specs=[VMEM] * len(outs),
        scratch_shapes=list(scratch),
        compiler_params=pltpu.CompilerParams(vmem_limit_bytes=60 * 1024 * 1024),
        cost_estimate=pl.CostEstimate(
            flops=int(COST[name] * 1e11), transcendentals=0, bytes_accessed=0
        ),
        name=name,
    )(*args)


def at(start, size):
    return pl.ds(pl.multiple_of(start, size), size)


def chunk_cols(y, off):
    return at(lax.rem(y + (off + 4), 4) * CH, CH)


def row_parts(r):
    e = (r * 2731) >> 16
    q = r - e * GROUP
    core = q >= CAP
    return e, core, jnp.where(core, q - CAP, q)


def slot_key(ids):
    e = iota((EXPERTS, 128), 0)
    member = jnp.zeros((EXPERTS, 128), F32)
    for k in range(TOP):
        member = member + onehot(ids[k : k + 1, :] == e)
    upto = onehot(iota((128, 128), 0) <= iota((128, 128), 1)).astype(BF)
    rank = mm(member.astype(BF), upto) - 1.0
    return jnp.where(member > 0.5, rank, F32(-1.0))


def slot_weight(ids, comb):
    e = iota((EXPERTS, 128), 0)
    out = jnp.zeros((EXPERTS, 128), F32)
    for k in range(TOP):
        out = out + jnp.where(ids[k : k + 1, :] == e, comb[k : k + 1, :], F32(0.0))
    return out.astype(BF)


def expert_rows():
    e, _, _ = row_parts(iota((ROWS, EXPERTS), 0))
    return onehot(e == iota((ROWS, EXPERTS), 1)).astype(BF)


def got_ids(pk):
    return pk[256:272, :128].astype(F32)[:8].astype(I32)


def pack_body(pos, ids, comb, tokens, grads, out):
    cols = at((1 - pos[1]) * HALF + pos[0] * CH, CH)
    out[:128, :] = tokens[:, cols]
    out[128:256, :] = grads[:, cols]
    row = jnp.concatenate(
        [ids[...].astype(F32), comb[...].astype(F32), jnp.zeros((8, 256), F32)], axis=1
    )
    out[256:, :] = jnp.concatenate([row, jnp.zeros((8, CH), F32)], axis=0).astype(BF)


def send_body(weighted, pos, ids, comb, pk, rows_ref, out):
    y, h = pos[0], pos[1]
    rows = expert_rows()
    _, core, slot = row_parts(iota((ROWS, 128), 0))
    slot = slot.astype(F32)
    parts = []
    for mine, idv, cv in (
        (True, ids[...], comb[...].astype(F32)),
        (False, got_ids(pk), pk[256:272, 128:256].astype(F32)[:8]),
    ):
        key = mm(rows, slot_key(idv).astype(BF))
        member = (key == slot) & (core == ((h == 1) if mine else (h == 0)))
        if weighted:
            parts.append(jnp.where(member, mm(rows, slot_weight(idv, cv)), F32(0.0)))
        else:
            parts.append(onehot(member))
    lhs = jnp.concatenate(parts, axis=1).astype(BF)
    got = pk[128:256, :] if weighted else pk[:128, :]
    rhs = jnp.concatenate([rows_ref[:, at(h * HALF + y * CH, CH)], got], axis=0)
    out[...] = mm(lhs, rhs).astype(BF)


def weight_send_body(pos, gw, uw, dw, out):
    other = at((1 - pos[1]) * HALF, HALF)
    for m, w in enumerate((gw, uw, dw)):
        out[m] = w[:, other]


def weight_join_body(pos, gw, uw, dw, got, gu, down):
    h = pos[1]
    for m, w in enumerate((gw, uw)):
        gu[m, at(h * 192, 192), :] = w[:, at(h * HALF, HALF)]
        gu[m, at((1 - h) * 192, 192), :] = got[m]
    down[at(h * 192, 192), :] = dw[:, at(h * HALF, HALF)]
    down[at((1 - h) * 192, 192), :] = got[2]


def unit_weights(w, y, off):
    return w[:, :, chunk_cols(y, off)].reshape(2 * UNITS, CH)


def gate_up_body(pos, x0, x1, x2, xa, xb, w, out):
    y = pos[0]

    def block(i, carry):
        rs = at(i * 256, 256)
        acc = None
        for x, off in zip((x0, x1, x2), OFFS[:3]):
            part = mm(x[rs, :], unit_weights(w, y, off), NT)
            acc = part if acc is None else acc + part
        out[rs, :] = acc
        return carry

    lax.fori_loop(0, 3, block, 0)
    wc = unit_weights(w, y, 2)
    out[:HR, :] += mm(xa[...], wc, NT)
    out[HR:, :] += mm(xb[...], wc, NT)


def back_near_body(pos, *refs):
    a, b, la, lb, rb, ra, w, out = refs
    for half, xs in enumerate(((a, la, ra), (b, lb, rb))):
        acc = None
        for x, off in zip(xs, OFFS[:3]):
            part = mm(x[...], w[:, chunk_cols(pos[0], off)], NT)
            acc = part if acc is None else acc + part
        out[half * HR : (half + 1) * HR, :] = acc


def back_body(pos, acc, xa, xb, w, out):
    wc = w[:, chunk_cols(pos[0], 2)]
    out[:HR, :] = acc[:HR, :] + mm(xa[...], wc, NT)
    out[HR:, :] = acc[HR:, :] + mm(xb[...], wc, NT)


def input_part(both, w, y, off):
    wc = unit_weights(w, y, off)
    return (mm(both[...], wc) * (2 * FF) ** (-0.5)).astype(BF)


def mid_body(pos, gu_a, gu_b, bk_a, bk_b, w, both, hd, cb, d2a, d2b):
    y, h = pos[0], pos[1]
    scale = D**-0.5
    own = (iota((128, UNITS), 1) >= 192) == (h == 1)

    def block(i, carry):
        rs = at(i * 128, 128)
        gate = (gu_a[rs, :UNITS] + gu_b[rs, :UNITS]) * scale
        up = (gu_a[rs, UNITS:] + gu_b[rs, UNITS:]) * scale
        back = bk_a[rs, :] + bk_b[rs, :]
        sig = jax.nn.sigmoid(gate)
        active = gate * sig
        hidden = active * up
        slope = sig * (1.0 + gate * (1.0 - sig))
        scaled = back * scale
        both[rs, :UNITS] = (scaled * up * slope).astype(BF)
        both[rs, UNITS:] = (scaled * active).astype(BF)
        hd[rs, :] = hidden.astype(BF)
        c = jnp.sum(jnp.where(own, hidden * back, F32(0.0)), axis=1, keepdims=True)
        cb[rs, :] = jnp.broadcast_to(c * (D * FF) ** (-0.5), (128, 128)).astype(BF)
        return carry

    lax.fori_loop(0, 6, block, 0)
    part = input_part(both, w, y, 2)
    d2a[...] = part[:HR]
    d2b[...] = part[HR:]


def rest_body(pos, both, w, dpa, dpb, dma, dmb, d0):
    y = pos[0]
    for off, (top, bottom) in ((1, (dpa, dpb)), (-1, (dma, dmb))):
        part = input_part(both, w, y, off)
        top[...] = part[:HR]
        bottom[...] = part[HR:]
    d0[...] = input_part(both, w, y, 0)


def pass_on_body(pos, dpa, r2, dmb, q2, pa, mb):
    pa[...] = (dpa[...].astype(F32) + r2[...].astype(F32)).astype(BF)
    mb[...] = (dmb[...].astype(F32) + q2[...].astype(F32)).astype(BF)


def finish_body(pos, d0, ma, pa, mb, pb, out):
    for rs, a, b in ((slice(0, HR), ma, pa), (slice(HR, ROWS), mb, pb)):
        total = d0[rs, :].astype(F32) + a[...].astype(F32) + b[...].astype(F32)
        out[rs, :] = total.astype(BF)


def wgrad(pos, half, gu_t, hd_t, xs, gs, store):
    y = pos[0]
    rows = at(half * 192, 192)
    lhs = gu_t[:, rows, :].reshape(2 * 192, ROWS)
    low = hd_t[rows, :]
    factor = 512.0 ** (-0.5)
    for i, off in enumerate(OFFS):
        if i < 3:
            part = mm(lhs, xs[i][...])
        else:
            part = mm(lhs[:, :HR], xs[3][...]) + mm(lhs[:, HR:], xs[4][...])
        last = mm(low[:, :HR], gs[2 * i][...]) + mm(low[:, HR:], gs[2 * i + 1][...])
        part = (part * factor).astype(BF)
        c = lax.rem(y + (off + 4), 4) * CH
        store(0, c, part[:192])
        store(1, c, part[192:])
        store(2, c, (last * factor).astype(BF))


def wgrad_body(first, pos, both, hd, *refs):
    xs, gs, (out, gu_t, hd_t) = refs[:5], refs[5:13], refs[13:]
    h = pos[1]
    for m in range(2):
        gu_t[m] = both[:, m * UNITS : (m + 1) * UNITS].T
    hd_t[...] = hd[...].T

    def store(m, c, part):
        out[m, :, at(c, CH)] = part

    wgrad(pos, 1 - h if first else h, gu_t, hd_t, xs, gs, store)


def wgrad_join_body(pos, own, got, *outs):
    h = pos[1]
    for m in range(3):
        outs[m][:, at(h * HALF, HALF)] = own[m]
        outs[m][:, at((1 - h) * HALF, HALF)] = got[m]


def hi_lo(x):
    hi = x.astype(BF).astype(F32)
    wide = jnp.concatenate([hi, x - hi], axis=0)
    return jnp.concatenate([wide, jnp.zeros((16, CH - 128), F32)], axis=1).astype(BF)


def collect_body(pos, ids, pk, r, cb, q, sib):
    h = pos[1]
    pair = (ids[...], got_ids(pk))
    key = jnp.concatenate([slot_key(i).T for i in pair], axis=0).astype(BF)
    rows = expert_rows()
    key = mm(key, rows, NT)
    _, core, slot = row_parts(iota((256, ROWS), 1))
    core = core == ((iota((256, ROWS), 0) >= 128) != (h == 1))
    lhs = onehot((key == slot.astype(F32)) & core).astype(BF)
    acc = mm(lhs, r[...])
    q[:128, :] = acc[:128].astype(BF)
    sib[:128, :] = acc[128:].astype(BF)
    tokw = mm(lhs, (cb[:, :EXPERTS].astype(F32) * rows.astype(F32)).astype(BF))
    e = iota((EXPERTS, 128), 0)
    sums = []
    for b, idv in enumerate(pair):
        tw = tokw[b * 128 : (b + 1) * 128].T
        picked = [
            jnp.sum(jnp.where(idv[k : k + 1, :] == e, tw, F32(0.0)), axis=0, keepdims=True)
            for k in range(TOP)
        ]
        sums.append(jnp.concatenate(picked, axis=0))
    q[128:, :] = hi_lo(sums[0])
    sib[128:, :] = hi_lo(sums[1])


def assemble_body(pos, comb, *refs):
    parts, (out, cg) = refs[:8], refs[8:]
    y, h = pos[0], pos[1]
    total = jnp.zeros((16, 128), F32)
    for i, off in enumerate(OFFS):
        c = lax.rem(y + (off + 4), 4) * CH
        a, b = parts[2 * i], parts[2 * i + 1]
        out[:, at(h * HALF + c, CH)] = a[:128, :]
        out[:, at((1 - h) * HALF + c, CH)] = b[:128, :]
        total = total + a[128:144, :128].astype(F32) + b[128:144, :128].astype(F32)
    cg[...] = (total[:8] + total[8:]) / comb[...].astype(F32)


def on_device(tokens, out_grad, expert_ids, combine, gate_weight, up_weight, down_weight):
    n_dp = lax.axis_size("dp")
    width = lax.axis_size("expert")
    up_ring = [(i, (i + 1) % n_dp) for i in range(n_dp)]
    down_ring = [(i, (i - 1) % n_dp) for i in range(n_dp)]
    cores = [(i, i ^ 1) for i in range(width)]
    same_core = [list(range(c, width, 2)) for c in range(2)]

    def up(x):
        return lax.ppermute(x, "dp", up_ring)

    def down(x):
        return lax.ppermute(x, "dp", down_ring)

    def swap(x):
        return lax.ppermute(x, "expert", cores)

    def exchange(x):
        n = x.shape[1]
        x = x.reshape(EXPERTS, GROUP, n)
        x = lax.all_to_all(
            x, "expert", split_axis=0, concat_axis=0, axis_index_groups=same_core, tiled=True
        )
        return x.reshape(ROWS, n)

    def spread(x):
        left, right = up(x), down(x)
        return x, left, right, up(left[:HR]), down(right[HR:])

    def spread_halves(a, b):
        la, rb, lb, ra = up(a), down(b), up(b), down(a)
        return a, b, la, lb, ra, rb, up(la), down(rb)

    tie = lax.optimization_barrier
    pos = jnp.stack([lax.axis_index("dp"), lax.axis_index("expert") & 1]).astype(I32)
    ids = expert_ids.T
    comb = combine.T
    gw, uw, dw = gate_weight[0], up_weight[0], down_weight[0]

    (pk,) = call(
        pack_body, [((272, CH), BF)], (pos, ids, comb, tokens, out_grad), name="pack"
    )
    pk = swap(pk)

    def send(weighted, rows):
        return call(
            functools.partial(send_body, weighted), [((ROWS, CH), BF)],
            (pos, ids, comb, pk, rows), name="send",
        )[0]

    xs, later = tie((send(False, tokens), pos))
    xs = exchange(xs)
    gs, xs = tie((send(True, out_grad), xs))
    gs = exchange(gs)
    (wsend,) = call(
        weight_send_body, [((3, 192, HALF), BF)], (later, gw, uw, dw), name="weight_send"
    )
    wgot = swap(wsend)
    wgu, wd = call(
        weight_join_body, [((2, UNITS, HALF), BF), ((UNITS, HALF), BF)],
        (pos, gw, uw, dw, wgot), name="weight_join",
    )
    xs, gs = spread(xs), list(spread_halves(gs[:HR], gs[HR:]))
    (gu_a,) = call(gate_up_body, [((ROWS, 2 * UNITS), F32)], (pos, *xs, wgu), name="gate_up")
    gu_b = swap(gu_a)
    (bk_a,) = call(
        back_near_body, [((ROWS, UNITS), F32)], (pos, *gs[:4], gs[5], gs[4], wd), name="back_near"
    )
    (bk_a,) = call(
        back_body, [((ROWS, UNITS), F32)], (pos, bk_a, *gs[6:], wd), name="back"
    )
    bk_b = swap(bk_a)
    both, hd, cb, d2a, d2b = call(
        mid_body,
        [((ROWS, 2 * UNITS), BF), ((ROWS, UNITS), BF), ((ROWS, 128), BF)]
        + [((HR, CH), BF)] * 2,
        (pos, gu_a, gu_b, bk_a, bk_b, wgu), name="mid",
    )
    r2, q2 = up(d2a), down(d2b)
    dpa, dpb, dma, dmb, d0 = call(
        rest_body, [((HR, CH), BF)] * 4 + [((ROWS, CH), BF)], (pos, both, wgu), name="rest"
    )
    pb, ma = up(dpb), down(dma)
    pa, mb = call(pass_on_body, [((HR, CH), BF)] * 2, (pos, dpa, r2, dmb, q2), name="pass_on")
    pa, mb = up(pa), down(mb)
    pb, cb = tie((pb, cb))
    cb = exchange(cb)
    (r,) = call(finish_body, [((ROWS, CH), BF)], (pos, d0, ma, pa, mb, pb), name="finish")
    both, r, cb = tie((both, r, cb))
    r = exchange(r)
    def weight_grads(first):
        return call(
            functools.partial(wgrad_body, first), [((3, 192, HALF), BF)],
            (pos, both, hd, *xs, *gs),
            scratch=[pltpu.VMEM((2, UNITS, ROWS), BF), pltpu.VMEM((UNITS, ROWS), BF)],
            name="wgrad",
        )[0]

    dgot = swap(weight_grads(True))
    w_own = weight_grads(False)
    r, w_own = tie((r, w_own))
    qa, sib = call(
        collect_body, [((144, CH), BF)] * 2, (pos, ids, pk, r, cb), name="collect"
    )
    qb = swap(sib)
    parts = spread_halves(qa, qb)
    qb, w_own = tie((qb, w_own))
    dwg, dwu, dwd = call(
        wgrad_join_body, [((192, D), BF)] * 3, (pos, w_own, dgot), name="wgrad_join"
    )
    comb, dwg = tie((comb, dwg))
    input_grad, cg = call(
        assemble_body, [((128, D), BF), ((TOP, 128), F32)], (pos, comb, *parts), name="assemble"
    )
    return (input_grad, cg.T, dwg[None], dwu[None], dwd[None])


def solution(mesh):
    rows = P("expert", None)
    units = P("expert", "dp", None)
    return jax.shard_map(
        on_device,
        mesh=mesh,
        in_specs=(rows, rows, rows, rows, units, units, units),
        out_specs=(rows, rows, units, units, units),
        check_vma=False,
    )
```

```python
import functools

import jax
import jax.numpy as jnp
from jax import lax
from jax.experimental import pallas as pl
from jax.experimental.pallas import tpu as pltpu
from jax.sharding import PartitionSpec as P

D = 4096
FF = 1536
TOP = 8
EXPERTS = 32
BF = jnp.bfloat16
F32 = jnp.float32
I32 = jnp.int32
HALF = D // 2
CH = 512
CAP = 12
GROUP = 2 * CAP
ROWS = EXPERTS * GROUP
UNITS = 384
NT = (((1,), (1,)), ((), ()))
NN = (((1,), (0,)), ((), ()))
HR = ROWS // 2
OFFS = (0, -1, 1, 2)

SMEM = pl.BlockSpec(memory_space=pltpu.SMEM)
VMEM = pl.BlockSpec(memory_space=pltpu.VMEM)


def mm(a, b, dims=NN):
    return lax.dot_general(a, b, dims, preferred_element_type=F32)


def iota(shape, axis):
    return lax.broadcasted_iota(I32, shape, axis)


def onehot(mask):
    return jnp.where(mask, F32(1.0), F32(0.0))


COST = {
    "pack": 2, "send": 3, "weight_send": 4, "weight_join": 6, "gate_up": 8, "back_near": 5, "back": 3,
    "mid": 8, "rest": 4, "pass_on": 2,
    "wgrad": 13, "wgrad_join": 5, "finish": 2, "collect": 3, "assemble": 2,
}


def call(body, outs, args, scratch=(), name=None):
    return pl.pallas_call(
        body,
        out_shape=[jax.ShapeDtypeStruct(s, t) for s, t in outs],
        in_specs=[SMEM] + [VMEM] * (len(args) - 1),
        out_specs=[VMEM] * len(outs),
        scratch_shapes=list(scratch),
        compiler_params=pltpu.CompilerParams(vmem_limit_bytes=40 * 1024 * 1024),
        cost_estimate=pl.CostEstimate(
            flops=COST[name] * 100_000_000_000, transcendentals=0, bytes_accessed=0
        ),
        name=name,
    )(*args)


def at(start, size):
    return pl.ds(pl.multiple_of(start, size), size)


def chunk_cols(y, off):
    return at(lax.rem(y + (off + 4), 4) * CH, CH)


def row_parts(r):
    e = (r * 2731) >> 16
    q = r - e * GROUP
    core = q >= CAP
    return e, core, jnp.where(core, q - CAP, q)


def slot_key(ids):
    e = iota((EXPERTS, 128), 0)
    member = jnp.zeros((EXPERTS, 128), F32)
    for k in range(TOP):
        member = member + onehot(ids[k : k + 1, :] == e)
    upto = onehot(iota((128, 128), 0) <= iota((128, 128), 1)).astype(BF)
    rank = mm(member.astype(BF), upto) - 1.0
    return jnp.where(member > 0.5, rank, F32(-1.0))


def slot_weight(ids, comb):
    e = iota((EXPERTS, 128), 0)
    out = jnp.zeros((EXPERTS, 128), F32)
    for k in range(TOP):
        out = out + jnp.where(ids[k : k + 1, :] == e, comb[k : k + 1, :], F32(0.0))
    return out.astype(BF)


def expert_rows():
    e, _, _ = row_parts(iota((ROWS, EXPERTS), 0))
    return onehot(e == iota((ROWS, EXPERTS), 1)).astype(BF)


def got_ids(pk):
    return pk[256:272, :128].astype(F32)[:8].astype(I32)


def pack_body(pos, ids, comb, tokens, grads, out):
    cols = at((1 - pos[1]) * HALF + pos[0] * CH, CH)
    out[:128, :] = tokens[:, cols]
    out[128:256, :] = grads[:, cols]
    row = jnp.concatenate(
        [ids[...].astype(F32), comb[...].astype(F32), jnp.zeros((8, 256), F32)], axis=1
    )
    out[256:, :] = jnp.concatenate([row, jnp.zeros((8, CH), F32)], axis=0).astype(BF)


def send_body(weighted, pos, ids, comb, pk, rows_ref, out):
    y, h = pos[0], pos[1]
    rows = expert_rows()
    _, core, slot = row_parts(iota((ROWS, 128), 0))
    slot = slot.astype(F32)
    parts = []
    for mine, idv, cv in (
        (True, ids[...], comb[...].astype(F32)),
        (False, got_ids(pk), pk[256:272, 128:256].astype(F32)[:8]),
    ):
        key = mm(rows, slot_key(idv).astype(BF))
        member = (key == slot) & (core == ((h == 1) if mine else (h == 0)))
        if weighted:
            parts.append(jnp.where(member, mm(rows, slot_weight(idv, cv)), F32(0.0)))
        else:
            parts.append(onehot(member))
    lhs = jnp.concatenate(parts, axis=1).astype(BF)
    got = pk[128:256, :] if weighted else pk[:128, :]
    rhs = jnp.concatenate([rows_ref[:, at(h * HALF + y * CH, CH)], got], axis=0)
    out[...] = mm(lhs, rhs).astype(BF)


def weight_send_body(pos, gw, uw, dw, out):
    other = at((1 - pos[1]) * HALF, HALF)
    for m, w in enumerate((gw, uw, dw)):
        out[m] = w[:, other]


def weight_join_body(pos, gw, uw, dw, got, gu, down):
    h = pos[1]
    for m, w in enumerate((gw, uw)):
        gu[m, at(h * 192, 192), :] = w[:, at(h * HALF, HALF)]
        gu[m, at((1 - h) * 192, 192), :] = got[m]
    down[at(h * 192, 192), :] = dw[:, at(h * HALF, HALF)]
    down[at((1 - h) * 192, 192), :] = got[2]


def unit_weights(w, y, off):
    return w[:, :, chunk_cols(y, off)].reshape(2 * UNITS, CH)


def gate_up_body(pos, x0, x1, x2, xa, xb, w, out):
    y = pos[0]

    def block(i, carry):
        rs = at(i * 256, 256)
        acc = None
        for x, off in zip((x0, x1, x2), OFFS[:3]):
            part = mm(x[rs, :], unit_weights(w, y, off), NT)
            acc = part if acc is None else acc + part
        out[rs, :] = acc
        return carry

    lax.fori_loop(0, 3, block, 0)
    wc = unit_weights(w, y, 2)
    out[:HR, :] += mm(xa[...], wc, NT)
    out[HR:, :] += mm(xb[...], wc, NT)


def back_near_body(pos, *refs):
    xs, w, out = refs[:6], refs[6], refs[7]
    for half in range(2):
        acc = None
        for x, off in zip(xs[half::2], OFFS[:3]):
            part = mm(x[...], w[:, chunk_cols(pos[0], off)], NT)
            acc = part if acc is None else acc + part
        out[half * HR : (half + 1) * HR, :] = acc


def back_body(pos, acc, xa, xb, w, out):
    wc = w[:, chunk_cols(pos[0], 2)]
    out[:HR, :] = acc[:HR, :] + mm(xa[...], wc, NT)
    out[HR:, :] = acc[HR:, :] + mm(xb[...], wc, NT)


def input_part(both, w, y, off):
    wc = unit_weights(w, y, off)
    return (mm(both[...], wc) * (2 * FF) ** (-0.5)).astype(BF)


def mid_body(pos, gu_a, gu_b, bk_a, bk_b, w, both, hd, cb, d2a, d2b):
    y, h = pos[0], pos[1]
    scale = D**-0.5
    own = (iota((128, UNITS), 1) >= 192) == (h == 1)

    def block(i, carry):
        rs = at(i * 128, 128)
        gate = (gu_a[rs, :UNITS] + gu_b[rs, :UNITS]) * scale
        up = (gu_a[rs, UNITS:] + gu_b[rs, UNITS:]) * scale
        back = bk_a[rs, :] + bk_b[rs, :]
        sig = jax.nn.sigmoid(gate)
        active = gate * sig
        hidden = active * up
        slope = sig * (1.0 + gate * (1.0 - sig))
        scaled = back * scale
        both[rs, :UNITS] = (scaled * up * slope).astype(BF)
        both[rs, UNITS:] = (scaled * active).astype(BF)
        hd[rs, :] = hidden.astype(BF)
        c = jnp.sum(jnp.where(own, hidden * back, F32(0.0)), axis=1, keepdims=True)
        cb[rs, :] = jnp.broadcast_to(c * (D * FF) ** (-0.5), (128, 128)).astype(BF)
        return carry

    lax.fori_loop(0, 6, block, 0)
    part = input_part(both, w, y, 2)
    d2a[...] = part[:HR]
    d2b[...] = part[HR:]


def rest_body(pos, both, w, dpa, dpb, dma, dmb, d0):
    y = pos[0]
    for off, (top, bottom) in ((1, (dpa, dpb)), (-1, (dma, dmb))):
        part = input_part(both, w, y, off)
        top[...] = part[:HR]
        bottom[...] = part[HR:]
    d0[...] = input_part(both, w, y, 0)


def pass_on_body(pos, dpa, r2, dmb, q2, pa, mb):
    pa[...] = (dpa[...].astype(F32) + r2[...].astype(F32)).astype(BF)
    mb[...] = (dmb[...].astype(F32) + q2[...].astype(F32)).astype(BF)


def finish_body(pos, d0, ma, pa, mb, pb, out):
    for rs, a, b in ((slice(0, HR), ma, pa), (slice(HR, ROWS), mb, pb)):
        total = d0[rs, :].astype(F32) + a[...].astype(F32) + b[...].astype(F32)
        out[rs, :] = total.astype(BF)


def wgrad(pos, half, gu_t, hd_t, xs, gs, store):
    y = pos[0]
    rows = at(half * 192, 192)
    lhs = gu_t[:, rows, :].reshape(2 * 192, ROWS)
    low = hd_t[rows, :]
    factor = 512.0 ** (-0.5)
    for i, off in enumerate(OFFS):
        if i < 3:
            part = mm(lhs, xs[i][...])
        else:
            part = mm(lhs[:, :HR], xs[3][...]) + mm(lhs[:, HR:], xs[4][...])
        last = mm(low[:, :HR], gs[2 * i][...]) + mm(low[:, HR:], gs[2 * i + 1][...])
        part = (part * factor).astype(BF)
        c = lax.rem(y + (off + 4), 4) * CH
        store(0, c, part[:192])
        store(1, c, part[192:])
        store(2, c, (last * factor).astype(BF))


def wgrad_body(pos, both, hd, *refs):
    xs, gs, (own, other, gu_t, hd_t) = refs[:5], refs[5:13], refs[13:]
    h = pos[1]
    for m in range(2):
        gu_t[m] = both[:, m * UNITS : (m + 1) * UNITS].T
    hd_t[...] = hd[...].T
    for half, out in ((1 - h, other), (h, own)):

        def store(m, c, part, out=out):
            out[m, :, at(c, CH)] = part

        wgrad(pos, half, gu_t, hd_t, xs, gs, store)


def wgrad_join_body(pos, own, got, *outs):
    h = pos[1]
    for m in range(3):
        outs[m][:, at(h * HALF, HALF)] = own[m]
        outs[m][:, at((1 - h) * HALF, HALF)] = got[m]


def hi_lo(x):
    hi = x.astype(BF).astype(F32)
    wide = jnp.concatenate([hi, x - hi], axis=0)
    return jnp.concatenate([wide, jnp.zeros((16, CH - 128), F32)], axis=1).astype(BF)


def collect_body(pos, ids, pk, r, cb, q, sib):
    h = pos[1]
    pair = (ids[...], got_ids(pk))
    key = jnp.concatenate([slot_key(i).T for i in pair], axis=0).astype(BF)
    rows = expert_rows()
    key = mm(key, rows, NT)
    _, core, slot = row_parts(iota((256, ROWS), 1))
    core = core == ((iota((256, ROWS), 0) >= 128) != (h == 1))
    lhs = onehot((key == slot.astype(F32)) & core).astype(BF)
    acc = mm(lhs, r[...])
    q[:128, :] = acc[:128].astype(BF)
    sib[:128, :] = acc[128:].astype(BF)
    tokw = mm(lhs, (cb[:, :EXPERTS].astype(F32) * rows.astype(F32)).astype(BF))
    e = iota((EXPERTS, 128), 0)
    sums = []
    for b, idv in enumerate(pair):
        tw = tokw[b * 128 : (b + 1) * 128].T
        picked = [
            jnp.sum(jnp.where(idv[k : k + 1, :] == e, tw, F32(0.0)), axis=0, keepdims=True)
            for k in range(TOP)
        ]
        sums.append(jnp.concatenate(picked, axis=0))
    q[128:, :] = hi_lo(sums[0])
    sib[128:, :] = hi_lo(sums[1])


def assemble_body(pos, comb, *refs):
    parts, (out, cg) = refs[:8], refs[8:]
    y, h = pos[0], pos[1]
    total = jnp.zeros((16, 128), F32)
    for i, off in enumerate(OFFS):
        c = lax.rem(y + (off + 4), 4) * CH
        a, b = parts[2 * i], parts[2 * i + 1]
        out[:, at(h * HALF + c, CH)] = a[:128, :]
        out[:, at((1 - h) * HALF + c, CH)] = b[:128, :]
        total = total + a[128:144, :128].astype(F32) + b[128:144, :128].astype(F32)
    cg[...] = (total[:8] + total[8:]) / comb[...].astype(F32)


def on_device(tokens, out_grad, expert_ids, combine, gate_weight, up_weight, down_weight):
    n_dp = lax.axis_size("dp")
    width = lax.axis_size("expert")
    up_ring = [(i, (i + 1) % n_dp) for i in range(n_dp)]
    down_ring = [(i, (i - 1) % n_dp) for i in range(n_dp)]
    cores = [(i, i ^ 1) for i in range(width)]
    same_core = [list(range(c, width, 2)) for c in range(2)]

    def up(x):
        return lax.ppermute(x, "dp", up_ring)

    def down(x):
        return lax.ppermute(x, "dp", down_ring)

    def swap(x):
        return lax.ppermute(x, "expert", cores)

    def exchange(x):
        n = x.shape[1]
        x = x.reshape(EXPERTS, GROUP, n)
        x = lax.all_to_all(
            x, "expert", split_axis=0, concat_axis=0, axis_index_groups=same_core, tiled=True
        )
        return x.reshape(ROWS, n)

    def spread(x):
        left, right = up(x), down(x)
        return x, left, right, up(left[:HR]), down(right[HR:])

    def spread_halves(a, b):
        la, rb, lb, ra = up(a), down(b), up(b), down(a)
        return a, b, la, lb, ra, rb, up(la), down(rb)

    tie = lax.optimization_barrier
    pos = jnp.stack([lax.axis_index("dp"), lax.axis_index("expert") & 1]).astype(I32)
    ids = expert_ids.T
    comb = combine.T
    gw, uw, dw = gate_weight[0], up_weight[0], down_weight[0]

    (pk,) = call(
        pack_body, [((272, CH), BF)], (pos, ids, comb, tokens, out_grad), name="pack"
    )
    pk = swap(pk)

    def send(weighted, rows):
        return call(
            functools.partial(send_body, weighted), [((ROWS, CH), BF)],
            (pos, ids, comb, pk, rows), name="send",
        )[0]

    xs, later = tie((send(False, tokens), pos))
    xs = exchange(xs)
    gs, xs = tie((send(True, out_grad), xs))
    gs = exchange(gs)
    (wsend,) = call(
        weight_send_body, [((3, 192, HALF), BF)], (later, gw, uw, dw), name="weight_send"
    )
    wgot = swap(wsend)
    wgu, wd = call(
        weight_join_body, [((2, UNITS, HALF), BF), ((UNITS, HALF), BF)],
        (pos, gw, uw, dw, wgot), name="weight_join",
    )
    xs, gs = spread(xs), spread_halves(gs[:HR], gs[HR:])
    (gu_a,) = call(gate_up_body, [((ROWS, 2 * UNITS), F32)], (pos, *xs, wgu), name="gate_up")
    gu_b = swap(gu_a)
    (bk_a,) = call(
        back_near_body, [((ROWS, UNITS), F32)], (pos, *gs[:6], wd), name="back_near"
    )
    (bk_a,) = call(
        back_body, [((ROWS, UNITS), F32)], (pos, bk_a, *gs[6:], wd), name="back"
    )
    bk_b = swap(bk_a)
    both, hd, cb, d2a, d2b = call(
        mid_body,
        [((ROWS, 2 * UNITS), BF), ((ROWS, UNITS), BF), ((ROWS, 128), BF)]
        + [((HR, CH), BF)] * 2,
        (pos, gu_a, gu_b, bk_a, bk_b, wgu), name="mid",
    )
    r2, q2 = up(d2a), down(d2b)
    dpa, dpb, dma, dmb, d0 = call(
        rest_body, [((HR, CH), BF)] * 4 + [((ROWS, CH), BF)], (pos, both, wgu), name="rest"
    )
    pb, ma = up(dpb), down(dma)
    pa, mb = call(pass_on_body, [((HR, CH), BF)] * 2, (pos, dpa, r2, dmb, q2), name="pass_on")
    pa, mb = up(pa), down(mb)
    pb, cb = tie((pb, cb))
    cb = exchange(cb)
    (r,) = call(finish_body, [((ROWS, CH), BF)], (pos, d0, ma, pa, mb, pb), name="finish")
    both, r, cb = tie((both, r, cb))
    r = exchange(r)
    w_own, w_other = call(
        wgrad_body, [((3, 192, HALF), BF)] * 2, (pos, both, hd, *xs, *gs),
        scratch=[pltpu.VMEM((2, UNITS, ROWS), BF), pltpu.VMEM((UNITS, ROWS), BF)],
        name="wgrad",
    )
    r, w_other = tie((r, w_other))
    qa, sib = call(
        collect_body, [((144, CH), BF)] * 2, (pos, ids, pk, r, cb), name="collect"
    )
    la, ra = up(qa), down(qa)
    sib, la, ra = tie((sib, la, ra))
    qb, w_other = tie((swap(sib), w_other))
    dgot = swap(w_other)
    lb, rb = up(qb), down(qb)
    parts = (qa, qb, la, lb, ra, rb, up(la), down(rb))
    qb, w_own = tie((qb, w_own))
    dwg, dwu, dwd = call(
        wgrad_join_body, [((192, D), BF)] * 3, (pos, w_own, dgot), name="wgrad_join"
    )
    comb, dwg = tie((comb, dwg))
    input_grad, cg = call(
        assemble_body, [((128, D), BF), ((TOP, 128), F32)], (pos, comb, *parts), name="assemble"
    )
    return (input_grad, cg.T, dwg[None], dwu[None], dwd[None])


def solution(mesh):
    rows = P("expert", None)
    units = P("expert", "dp", None)
    return jax.shard_map(
        on_device,
        mesh=mesh,
        in_specs=(rows, rows, rows, rows, units, units, units),
        out_specs=(rows, rows, units, units, units),
        check_vma=False,
    )
```

```python
import functools

import jax
import jax.numpy as jnp
from jax import lax
from jax.experimental import pallas as pl
from jax.experimental.pallas import tpu as pltpu
from jax.sharding import PartitionSpec as P

D = 4096
FF = 1536
TOP = 8
EXPERTS = 32
BF = jnp.bfloat16
F32 = jnp.float32
I32 = jnp.int32
HALF = D // 2
CH = 512
CAP = 12
GROUP = 2 * CAP
ROWS = EXPERTS * GROUP
UNITS = 384
NT = (((1,), (1,)), ((), ()))
NN = (((1,), (0,)), ((), ()))
HR = ROWS // 2
OFFS = (0, -1, 1, 2)

SMEM = pl.BlockSpec(memory_space=pltpu.SMEM)
VMEM = pl.BlockSpec(memory_space=pltpu.VMEM)


def mm(a, b, dims=NN):
    return lax.dot_general(a, b, dims, preferred_element_type=F32)


def iota(shape, axis):
    return lax.broadcasted_iota(I32, shape, axis)


def onehot(mask):
    return jnp.where(mask, F32(1.0), F32(0.0))


COST = {
    "pack": 2, "send": 3, "weight_send": 4, "weight_join": 6, "gate_up": 8, "back_near": 5, "back": 3,
    "mid": 8, "rest": 4, "pass_on": 2,
    "wgrad": 13, "wgrad_join": 5, "finish": 2, "collect": 3, "assemble": 2,
}

CHAIN = ("back", "mid", "rest", "pass_on", "finish", "assemble", "gate_up", "back_near")


def call(body, outs, args, scratch=(), name=None):
    return pl.pallas_call(
        body,
        out_shape=[jax.ShapeDtypeStruct(s, t) for s, t in outs],
        in_specs=[SMEM] + [VMEM] * (len(args) - 1),
        out_specs=[VMEM] * len(outs),
        scratch_shapes=list(scratch),
        compiler_params=pltpu.CompilerParams(vmem_limit_bytes=(40 if name in CHAIN else 60) * 1024 * 1024),
        cost_estimate=pl.CostEstimate(
            flops=COST[name] * 100_000_000_000, transcendentals=0, bytes_accessed=0
        ),
        name=name,
    )(*args)


def at(start, size):
    return pl.ds(pl.multiple_of(start, size), size)


def chunk_cols(y, off):
    return at(lax.rem(y + (off + 4), 4) * CH, CH)


def row_parts(r):
    e = (r * 2731) >> 16
    q = r - e * GROUP
    core = q >= CAP
    return e, core, jnp.where(core, q - CAP, q)


def slot_key(ids):
    e = iota((EXPERTS, 128), 0)
    member = jnp.zeros((EXPERTS, 128), F32)
    for k in range(TOP):
        member = member + onehot(ids[k : k + 1, :] == e)
    upto = onehot(iota((128, 128), 0) <= iota((128, 128), 1)).astype(BF)
    rank = mm(member.astype(BF), upto) - 1.0
    return jnp.where(member > 0.5, rank, F32(-1.0))


def slot_weight(ids, comb):
    e = iota((EXPERTS, 128), 0)
    out = jnp.zeros((EXPERTS, 128), F32)
    for k in range(TOP):
        out = out + jnp.where(ids[k : k + 1, :] == e, comb[k : k + 1, :], F32(0.0))
    return out.astype(BF)


def expert_rows():
    e, _, _ = row_parts(iota((ROWS, EXPERTS), 0))
    return onehot(e == iota((ROWS, EXPERTS), 1)).astype(BF)


def got_ids(pk):
    return pk[256:272, :128].astype(F32)[:8].astype(I32)


def pack_body(pos, ids, comb, tokens, grads, out):
    cols = at((1 - pos[1]) * HALF + pos[0] * CH, CH)
    out[:128, :] = tokens[:, cols]
    out[128:256, :] = grads[:, cols]
    row = jnp.concatenate(
        [ids[...].astype(F32), comb[...].astype(F32), jnp.zeros((8, 256), F32)], axis=1
    )
    out[256:, :] = jnp.concatenate([row, jnp.zeros((8, CH), F32)], axis=0).astype(BF)


def send_body(weighted, pos, ids, comb, pk, rows_ref, out):
    y, h = pos[0], pos[1]
    rows = expert_rows()
    _, core, slot = row_parts(iota((ROWS, 128), 0))
    slot = slot.astype(F32)
    parts = []
    for mine, idv, cv in (
        (True, ids[...], comb[...].astype(F32)),
        (False, got_ids(pk), pk[256:272, 128:256].astype(F32)[:8]),
    ):
        key = mm(rows, slot_key(idv).astype(BF))
        member = (key == slot) & (core == ((h == 1) if mine else (h == 0)))
        if weighted:
            parts.append(jnp.where(member, mm(rows, slot_weight(idv, cv)), F32(0.0)))
        else:
            parts.append(onehot(member))
    lhs = jnp.concatenate(parts, axis=1).astype(BF)
    got = pk[128:256, :] if weighted else pk[:128, :]
    rhs = jnp.concatenate([rows_ref[:, at(h * HALF + y * CH, CH)], got], axis=0)
    out[...] = mm(lhs, rhs).astype(BF)


def weight_send_body(pos, gw, uw, dw, out):
    other = at((1 - pos[1]) * HALF, HALF)
    for m, w in enumerate((gw, uw, dw)):
        out[m] = w[:, other]


def weight_join_body(pos, gw, uw, dw, got, gu, down):
    h = pos[1]
    for m, w in enumerate((gw, uw)):
        gu[m, at(h * 192, 192), :] = w[:, at(h * HALF, HALF)]
        gu[m, at((1 - h) * 192, 192), :] = got[m]
    down[at(h * 192, 192), :] = dw[:, at(h * HALF, HALF)]
    down[at((1 - h) * 192, 192), :] = got[2]


def unit_weights(w, y, off):
    return w[:, :, chunk_cols(y, off)].reshape(2 * UNITS, CH)


def gate_up_body(pos, x0, x1, x2, xa, xb, w, out):
    y = pos[0]

    def block(i, carry):
        rs = at(i * 256, 256)
        acc = None
        for x, off in zip((x0, x1, x2), OFFS[:3]):
            part = mm(x[rs, :], unit_weights(w, y, off), NT)
            acc = part if acc is None else acc + part
        out[rs, :] = acc
        return carry

    lax.fori_loop(0, 3, block, 0)
    wc = unit_weights(w, y, 2)
    out[:HR, :] += mm(xa[...], wc, NT)
    out[HR:, :] += mm(xb[...], wc, NT)


def back_near_body(pos, *refs):
    xs, w, out = refs[:6], refs[6], refs[7]
    for half in range(2):
        acc = None
        for x, off in zip(xs[half::2], OFFS[:3]):
            part = mm(x[...], w[:, chunk_cols(pos[0], off)], NT)
            acc = part if acc is None else acc + part
        out[half * HR : (half + 1) * HR, :] = acc


def back_body(pos, acc, xa, xb, w, out):
    wc = w[:, chunk_cols(pos[0], 2)]
    out[:HR, :] = acc[:HR, :] + mm(xa[...], wc, NT)
    out[HR:, :] = acc[HR:, :] + mm(xb[...], wc, NT)


def input_part(both, w, y, off):
    wc = unit_weights(w, y, off)
    return (mm(both[...], wc) * (2 * FF) ** (-0.5)).astype(BF)


def mid_body(pos, gu_a, gu_b, bk_a, bk_b, w, both, hd, cb, d2a, d2b):
    y, h = pos[0], pos[1]
    scale = D**-0.5
    own = (iota((128, UNITS), 1) >= 192) == (h == 1)

    def block(i, carry):
        rs = at(i * 128, 128)
        gate = (gu_a[rs, :UNITS] + gu_b[rs, :UNITS]) * scale
        up = (gu_a[rs, UNITS:] + gu_b[rs, UNITS:]) * scale
        back = bk_a[rs, :] + bk_b[rs, :]
        sig = jax.nn.sigmoid(gate)
        active = gate * sig
        hidden = active * up
        slope = sig * (1.0 + gate * (1.0 - sig))
        scaled = back * scale
        both[rs, :UNITS] = (scaled * up * slope).astype(BF)
        both[rs, UNITS:] = (scaled * active).astype(BF)
        hd[rs, :] = hidden.astype(BF)
        c = jnp.sum(jnp.where(own, hidden * back, F32(0.0)), axis=1, keepdims=True)
        cb[rs, :] = jnp.broadcast_to(c * (D * FF) ** (-0.5), (128, 128)).astype(BF)
        return carry

    lax.fori_loop(0, 6, block, 0)
    part = input_part(both, w, y, 2)
    d2a[...] = part[:HR]
    d2b[...] = part[HR:]


def rest_body(pos, both, w, dpa, dpb, dma, dmb, d0):
    y = pos[0]
    for off, (top, bottom) in ((1, (dpa, dpb)), (-1, (dma, dmb))):
        part = input_part(both, w, y, off)
        top[...] = part[:HR]
        bottom[...] = part[HR:]
    d0[...] = input_part(both, w, y, 0)


def pass_on_body(pos, dpa, r2, dmb, q2, pa, mb):
    pa[...] = (dpa[...].astype(F32) + r2[...].astype(F32)).astype(BF)
    mb[...] = (dmb[...].astype(F32) + q2[...].astype(F32)).astype(BF)


def finish_body(pos, d0, ma, pa, mb, pb, out):
    for rs, a, b in ((slice(0, HR), ma, pa), (slice(HR, ROWS), mb, pb)):
        total = d0[rs, :].astype(F32) + a[...].astype(F32) + b[...].astype(F32)
        out[rs, :] = total.astype(BF)


def wgrad(pos, half, gu_t, hd_t, xs, gs, store):
    y = pos[0]
    rows = at(half * 192, 192)
    lhs = gu_t[:, rows, :].reshape(2 * 192, ROWS)
    low = hd_t[rows, :]
    factor = 512.0 ** (-0.5)
    for i, off in enumerate(OFFS):
        if i < 3:
            part = mm(lhs, xs[i][...])
        else:
            part = mm(lhs[:, :HR], xs[3][...]) + mm(lhs[:, HR:], xs[4][...])
        last = mm(low[:, :HR], gs[2 * i][...]) + mm(low[:, HR:], gs[2 * i + 1][...])
        part = (part * factor).astype(BF)
        c = lax.rem(y + (off + 4), 4) * CH
        store(0, c, part[:192])
        store(1, c, part[192:])
        store(2, c, (last * factor).astype(BF))


def wgrad_body(pos, both, hd, *refs):
    xs, gs, (own, other, gu_t, hd_t) = refs[:5], refs[5:13], refs[13:]
    h = pos[1]
    for m in range(2):
        gu_t[m] = both[:, m * UNITS : (m + 1) * UNITS].T
    hd_t[...] = hd[...].T
    for half, out in ((1 - h, other), (h, own)):

        def store(m, c, part, out=out):
            out[m, :, at(c, CH)] = part

        wgrad(pos, half, gu_t, hd_t, xs, gs, store)


def wgrad_join_body(pos, own, got, *outs):
    h = pos[1]
    for m in range(3):
        outs[m][:, at(h * HALF, HALF)] = own[m]
        outs[m][:, at((1 - h) * HALF, HALF)] = got[m]


def hi_lo(x):
    hi = x.astype(BF).astype(F32)
    wide = jnp.concatenate([hi, x - hi], axis=0)
    return jnp.concatenate([wide, jnp.zeros((16, CH - 128), F32)], axis=1).astype(BF)


def collect_body(pos, ids, pk, r, cb, q, sib):
    h = pos[1]
    pair = (ids[...], got_ids(pk))
    key = jnp.concatenate([slot_key(i).T for i in pair], axis=0).astype(BF)
    rows = expert_rows()
    key = mm(key, rows, NT)
    _, core, slot = row_parts(iota((256, ROWS), 1))
    core = core == ((iota((256, ROWS), 0) >= 128) != (h == 1))
    lhs = onehot((key == slot.astype(F32)) & core).astype(BF)
    acc = mm(lhs, r[...])
    q[:128, :] = acc[:128].astype(BF)
    sib[:128, :] = acc[128:].astype(BF)
    tokw = mm(lhs, (cb[:, :EXPERTS].astype(F32) * rows.astype(F32)).astype(BF))
    e = iota((EXPERTS, 128), 0)
    sums = []
    for b, idv in enumerate(pair):
        tw = tokw[b * 128 : (b + 1) * 128].T
        picked = [
            jnp.sum(jnp.where(idv[k : k + 1, :] == e, tw, F32(0.0)), axis=0, keepdims=True)
            for k in range(TOP)
        ]
        sums.append(jnp.concatenate(picked, axis=0))
    q[128:, :] = hi_lo(sums[0])
    sib[128:, :] = hi_lo(sums[1])


def assemble_body(pos, comb, *refs):
    parts, (out, cg) = refs[:8], refs[8:]
    y, h = pos[0], pos[1]
    total = jnp.zeros((16, 128), F32)
    for i, off in enumerate(OFFS):
        c = lax.rem(y + (off + 4), 4) * CH
        a, b = parts[2 * i], parts[2 * i + 1]
        out[:, at(h * HALF + c, CH)] = a[:128, :]
        out[:, at((1 - h) * HALF + c, CH)] = b[:128, :]
        total = total + a[128:144, :128].astype(F32) + b[128:144, :128].astype(F32)
    cg[...] = (total[:8] + total[8:]) / comb[...].astype(F32)


def on_device(tokens, out_grad, expert_ids, combine, gate_weight, up_weight, down_weight):
    n_dp = lax.axis_size("dp")
    width = lax.axis_size("expert")
    up_ring = [(i, (i + 1) % n_dp) for i in range(n_dp)]
    down_ring = [(i, (i - 1) % n_dp) for i in range(n_dp)]
    cores = [(i, i ^ 1) for i in range(width)]
    same_core = [list(range(c, width, 2)) for c in range(2)]

    def up(x):
        return lax.ppermute(x, "dp", up_ring)

    def down(x):
        return lax.ppermute(x, "dp", down_ring)

    def swap(x):
        return lax.ppermute(x, "expert", cores)

    def exchange(x):
        n = x.shape[1]
        x = x.reshape(EXPERTS, GROUP, n)
        x = lax.all_to_all(
            x, "expert", split_axis=0, concat_axis=0, axis_index_groups=same_core, tiled=True
        )
        return x.reshape(ROWS, n)

    def spread(x):
        left, right = up(x), down(x)
        return x, left, right, up(left[:HR]), down(right[HR:])

    def spread_halves(a, b):
        la, rb, lb, ra = up(a), down(b), up(b), down(a)
        return a, b, la, lb, ra, rb, up(la), down(rb)

    tie = lax.optimization_barrier
    pos = jnp.stack([lax.axis_index("dp"), lax.axis_index("expert") & 1]).astype(I32)
    ids = expert_ids.T
    comb = combine.T
    gw, uw, dw = gate_weight[0], up_weight[0], down_weight[0]

    (pk,) = call(
        pack_body, [((272, CH), BF)], (pos, ids, comb, tokens, out_grad), name="pack"
    )
    pk = swap(pk)

    def send(weighted, rows):
        return call(
            functools.partial(send_body, weighted), [((ROWS, CH), BF)],
            (pos, ids, comb, pk, rows), name="send",
        )[0]

    xs, later = tie((send(False, tokens), pos))
    xs = exchange(xs)
    gs, xs = tie((send(True, out_grad), xs))
    gs = exchange(gs)
    (wsend,) = call(
        weight_send_body, [((3, 192, HALF), BF)], (later, gw, uw, dw), name="weight_send"
    )
    wgot = swap(wsend)
    wgu, wd = call(
        weight_join_body, [((2, UNITS, HALF), BF), ((UNITS, HALF), BF)],
        (pos, gw, uw, dw, wgot), name="weight_join",
    )
    xs, gs = spread(xs), spread_halves(gs[:HR], gs[HR:])
    (gu_a,) = call(gate_up_body, [((ROWS, 2 * UNITS), F32)], (pos, *xs, wgu), name="gate_up")
    gu_b = swap(gu_a)
    (bk_a,) = call(
        back_near_body, [((ROWS, UNITS), F32)], (pos, *gs[:6], wd), name="back_near"
    )
    (bk_a,) = call(
        back_body, [((ROWS, UNITS), F32)], (pos, bk_a, *gs[6:], wd), name="back"
    )
    bk_b = swap(bk_a)
    both, hd, cb, d2a, d2b = call(
        mid_body,
        [((ROWS, 2 * UNITS), BF), ((ROWS, UNITS), BF), ((ROWS, 128), BF)]
        + [((HR, CH), BF)] * 2,
        (pos, gu_a, gu_b, bk_a, bk_b, wgu), name="mid",
    )
    r2, q2 = up(d2a), down(d2b)
    dpa, dpb, dma, dmb, d0 = call(
        rest_body, [((HR, CH), BF)] * 4 + [((ROWS, CH), BF)], (pos, both, wgu), name="rest"
    )
    pb, ma = up(dpb), down(dma)
    pa, mb = call(pass_on_body, [((HR, CH), BF)] * 2, (pos, dpa, r2, dmb, q2), name="pass_on")
    pa, mb = up(pa), down(mb)
    pb, cb = tie((pb, cb))
    cb = exchange(cb)
    (r,) = call(finish_body, [((ROWS, CH), BF)], (pos, d0, ma, pa, mb, pb), name="finish")
    both, r, cb = tie((both, r, cb))
    r = exchange(r)
    w_own, w_other = call(
        wgrad_body, [((3, 192, HALF), BF)] * 2, (pos, both, hd, *xs, *gs),
        scratch=[pltpu.VMEM((2, UNITS, ROWS), BF), pltpu.VMEM((UNITS, ROWS), BF)],
        name="wgrad",
    )
    r, w_other = tie((r, w_other))
    dgot = swap(w_other)
    qa, sib = call(
        collect_body, [((144, CH), BF)] * 2, (pos, ids, pk, r, cb), name="collect"
    )
    qb = swap(sib)
    parts = spread_halves(qa, qb)
    qb, w_own = tie((qb, w_own))
    dwg, dwu, dwd = call(
        wgrad_join_body, [((192, D), BF)] * 3, (pos, w_own, dgot), name="wgrad_join"
    )
    comb, dwg = tie((comb, dwg))
    input_grad, cg = call(
        assemble_body, [((128, D), BF), ((TOP, 128), F32)], (pos, comb, *parts), name="assemble"
    )
    return (input_grad, cg.T, dwg[None], dwu[None], dwd[None])


def solution(mesh):
    rows = P("expert", None)
    units = P("expert", "dp", None)
    return jax.shard_map(
        on_device,
        mesh=mesh,
        in_specs=(rows, rows, rows, rows, units, units, units),
        out_specs=(rows, rows, units, units, units),
        check_vma=False,
    )
```

```python
import functools

import jax
import jax.numpy as jnp
from jax import lax
from jax.experimental import pallas as pl
from jax.experimental.pallas import tpu as pltpu
from jax.sharding import PartitionSpec as P

D = 4096
FF = 1536
TOP = 8
EXPERTS = 32
BF = jnp.bfloat16
F32 = jnp.float32
I32 = jnp.int32
HALF = D // 2
CH = 512
CAP = 12
GROUP = 2 * CAP
ROWS = EXPERTS * GROUP
UNITS = 384
NT = (((1,), (1,)), ((), ()))
NN = (((1,), (0,)), ((), ()))
HR = ROWS // 2
OFFS = (0, -1, 1, 2)

SMEM = pl.BlockSpec(memory_space=pltpu.SMEM)
VMEM = pl.BlockSpec(memory_space=pltpu.VMEM)


def mm(a, b, dims=NN):
    return lax.dot_general(a, b, dims, preferred_element_type=F32)


def iota(shape, axis):
    return lax.broadcasted_iota(I32, shape, axis)


def onehot(mask):
    return jnp.where(mask, F32(1.0), F32(0.0))


COST = {
    "pack": 2, "send": 3, "weight_send": 4, "weight_join": 6, "gate_up": 8, "back_near": 5, "back": 3,
    "mid": 8, "rest": 4, "pass_on": 2,
    "wgrad": 13, "wgrad_join": 5, "finish": 2, "collect": 3, "assemble": 2,
}

CHAIN = ("back", "mid", "rest", "pass_on", "finish", "assemble", "gate_up", "back_near")


def call(body, outs, args, scratch=(), name=None):
    return pl.pallas_call(
        body,
        out_shape=[jax.ShapeDtypeStruct(s, t) for s, t in outs],
        in_specs=[SMEM] + [VMEM] * (len(args) - 1),
        out_specs=[VMEM] * len(outs),
        scratch_shapes=list(scratch),
        compiler_params=pltpu.CompilerParams(vmem_limit_bytes=(40 if name in CHAIN else 60) * 1024 * 1024),
        cost_estimate=pl.CostEstimate(
            flops=COST[name] * 100_000_000_000, transcendentals=0, bytes_accessed=0
        ),
        name=name,
    )(*args)


def at(start, size):
    return pl.ds(pl.multiple_of(start, size), size)


def chunk_cols(y, off):
    return at(lax.rem(y + (off + 4), 4) * CH, CH)


def row_parts(r):
    e = (r * 2731) >> 16
    q = r - e * GROUP
    core = q >= CAP
    return e, core, jnp.where(core, q - CAP, q)


def slot_key(ids):
    e = iota((EXPERTS, 128), 0)
    member = jnp.zeros((EXPERTS, 128), F32)
    for k in range(TOP):
        member = member + onehot(ids[k : k + 1, :] == e)
    upto = onehot(iota((128, 128), 0) <= iota((128, 128), 1)).astype(BF)
    rank = mm(member.astype(BF), upto) - 1.0
    return jnp.where(member > 0.5, rank, F32(-1.0))


def slot_weight(ids, comb):
    e = iota((EXPERTS, 128), 0)
    out = jnp.zeros((EXPERTS, 128), F32)
    for k in range(TOP):
        out = out + jnp.where(ids[k : k + 1, :] == e, comb[k : k + 1, :], F32(0.0))
    return out.astype(BF)


def expert_rows():
    e, _, _ = row_parts(iota((ROWS, EXPERTS), 0))
    return onehot(e == iota((ROWS, EXPERTS), 1)).astype(BF)


def got_ids(pk):
    return pk[256:272, :128].astype(F32)[:8].astype(I32)


def pack_body(pos, ids, comb, tokens, grads, out):
    cols = at((1 - pos[1]) * HALF + pos[0] * CH, CH)
    out[:128, :] = tokens[:, cols]
    out[128:256, :] = grads[:, cols]
    row = jnp.concatenate(
        [ids[...].astype(F32), comb[...].astype(F32), jnp.zeros((8, 256), F32)], axis=1
    )
    out[256:, :] = jnp.concatenate([row, jnp.zeros((8, CH), F32)], axis=0).astype(BF)


def send_body(weighted, pos, ids, comb, pk, rows_ref, out):
    y, h = pos[0], pos[1]
    rows = expert_rows()
    _, core, slot = row_parts(iota((ROWS, 128), 0))
    slot = slot.astype(F32)
    parts = []
    for mine, idv, cv in (
        (True, ids[...], comb[...].astype(F32)),
        (False, got_ids(pk), pk[256:272, 128:256].astype(F32)[:8]),
    ):
        key = mm(rows, slot_key(idv).astype(BF))
        member = (key == slot) & (core == ((h == 1) if mine else (h == 0)))
        if weighted:
            parts.append(jnp.where(member, mm(rows, slot_weight(idv, cv)), F32(0.0)))
        else:
            parts.append(onehot(member))
    lhs = jnp.concatenate(parts, axis=1).astype(BF)
    got = pk[128:256, :] if weighted else pk[:128, :]
    rhs = jnp.concatenate([rows_ref[:, at(h * HALF + y * CH, CH)], got], axis=0)
    out[...] = mm(lhs, rhs).astype(BF)


def weight_send_body(pos, gw, uw, dw, out):
    other = at((1 - pos[1]) * HALF, HALF)
    for m, w in enumerate((gw, uw, dw)):
        out[m] = w[:, other]


def weight_join_body(pos, gw, uw, dw, got, gu, down):
    h = pos[1]
    for m, w in enumerate((gw, uw)):
        gu[m, at(h * 192, 192), :] = w[:, at(h * HALF, HALF)]
        gu[m, at((1 - h) * 192, 192), :] = got[m]
    down[at(h * 192, 192), :] = dw[:, at(h * HALF, HALF)]
    down[at((1 - h) * 192, 192), :] = got[2]


def unit_weights(w, y, off):
    return w[:, :, chunk_cols(y, off)].reshape(2 * UNITS, CH)


def gate_up_body(pos, x0, x1, x2, xa, xb, w, out):
    y = pos[0]

    def block(i, carry):
        rs = at(i * 256, 256)
        acc = None
        for x, off in zip((x0, x1, x2), OFFS[:3]):
            part = mm(x[rs, :], unit_weights(w, y, off), NT)
            acc = part if acc is None else acc + part
        out[rs, :] = acc
        return carry

    lax.fori_loop(0, 3, block, 0)
    wc = unit_weights(w, y, 2)
    out[:HR, :] += mm(xa[...], wc, NT)
    out[HR:, :] += mm(xb[...], wc, NT)


def back_near_body(pos, *refs):
    xs, w, out = refs[:6], refs[6], refs[7]
    for half in range(2):
        acc = None
        for x, off in zip(xs[half::2], OFFS[:3]):
            part = mm(x[...], w[:, chunk_cols(pos[0], off)], NT)
            acc = part if acc is None else acc + part
        out[half * HR : (half + 1) * HR, :] = acc


def back_body(pos, acc, xa, xb, w, out):
    wc = w[:, chunk_cols(pos[0], 2)]
    out[:HR, :] = acc[:HR, :] + mm(xa[...], wc, NT)
    out[HR:, :] = acc[HR:, :] + mm(xb[...], wc, NT)


def input_part(both, w, y, off):
    wc = unit_weights(w, y, off)
    return (mm(both[...], wc) * (2 * FF) ** (-0.5)).astype(BF)


def mid_body(pos, gu_a, gu_b, bk_a, bk_b, w, both, hd, cb, d2a, d2b):
    y, h = pos[0], pos[1]
    scale = D**-0.5
    own = (iota((128, UNITS), 1) >= 192) == (h == 1)

    def block(i, carry):
        rs = at(i * 128, 128)
        gate = (gu_a[rs, :UNITS] + gu_b[rs, :UNITS]) * scale
        up = (gu_a[rs, UNITS:] + gu_b[rs, UNITS:]) * scale
        back = bk_a[rs, :] + bk_b[rs, :]
        sig = jax.nn.sigmoid(gate)
        active = gate * sig
        hidden = active * up
        slope = sig * (1.0 + gate * (1.0 - sig))
        scaled = back * scale
        both[rs, :UNITS] = (scaled * up * slope).astype(BF)
        both[rs, UNITS:] = (scaled * active).astype(BF)
        hd[rs, :] = hidden.astype(BF)
        c = jnp.sum(jnp.where(own, hidden * back, F32(0.0)), axis=1, keepdims=True)
        cb[rs, :] = jnp.broadcast_to(c * (D * FF) ** (-0.5), (128, 128)).astype(BF)
        return carry

    lax.fori_loop(0, 6, block, 0)
    part = input_part(both, w, y, 2)
    d2a[...] = part[:HR]
    d2b[...] = part[HR:]


def rest_body(pos, both, w, dpa, dpb, dma, dmb, d0):
    y = pos[0]
    for off, (top, bottom) in ((1, (dpa, dpb)), (-1, (dma, dmb))):
        part = input_part(both, w, y, off)
        top[...] = part[:HR]
        bottom[...] = part[HR:]
    d0[...] = input_part(both, w, y, 0)


def pass_on_body(pos, dpa, r2, dmb, q2, pa, mb):
    pa[...] = (dpa[...].astype(F32) + r2[...].astype(F32)).astype(BF)
    mb[...] = (dmb[...].astype(F32) + q2[...].astype(F32)).astype(BF)


def finish_body(pos, d0, ma, pa, mb, pb, out):
    for rs, a, b in ((slice(0, HR), ma, pa), (slice(HR, ROWS), mb, pb)):
        total = d0[rs, :].astype(F32) + a[...].astype(F32) + b[...].astype(F32)
        out[rs, :] = total.astype(BF)


def wgrad(pos, half, gu_t, hd_t, xs, gs, store):
    y = pos[0]
    rows = at(half * 192, 192)
    lhs = gu_t[:, rows, :].reshape(2 * 192, ROWS)
    low = hd_t[rows, :]
    factor = 512.0 ** (-0.5)
    for i, off in enumerate(OFFS):
        if i < 3:
            part = mm(lhs, xs[i][...])
        else:
            part = mm(lhs[:, :HR], xs[3][...]) + mm(lhs[:, HR:], xs[4][...])
        last = mm(low[:, :HR], gs[2 * i][...]) + mm(low[:, HR:], gs[2 * i + 1][...])
        part = (part * factor).astype(BF)
        c = lax.rem(y + (off + 4), 4) * CH
        store(0, c, part[:192])
        store(1, c, part[192:])
        store(2, c, (last * factor).astype(BF))


def wgrad_body(pos, both, hd, *refs):
    xs, gs, (own, other, gu_t, hd_t) = refs[:5], refs[5:13], refs[13:]
    h = pos[1]
    for m in range(2):
        gu_t[m] = both[:, m * UNITS : (m + 1) * UNITS].T
    hd_t[...] = hd[...].T
    for half, out in ((1 - h, other), (h, own)):

        def store(m, c, part, out=out):
            out[m, :, at(c, CH)] = part

        wgrad(pos, half, gu_t, hd_t, xs, gs, store)


def wgrad_join_body(pos, own, got, *outs):
    h = pos[1]
    for m in range(3):
        outs[m][:, at(h * HALF, HALF)] = own[m]
        outs[m][:, at((1 - h) * HALF, HALF)] = got[m]


def hi_lo(x):
    hi = x.astype(BF).astype(F32)
    wide = jnp.concatenate([hi, x - hi], axis=0)
    return jnp.concatenate([wide, jnp.zeros((16, CH - 128), F32)], axis=1).astype(BF)


def collect_body(pos, ids, pk, r, cb, q, sib):
    h = pos[1]
    pair = (ids[...], got_ids(pk))
    key = jnp.concatenate([slot_key(i).T for i in pair], axis=0).astype(BF)
    rows = expert_rows()
    key = mm(key, rows, NT)
    _, core, slot = row_parts(iota((256, ROWS), 1))
    core = core == ((iota((256, ROWS), 0) >= 128) != (h == 1))
    lhs = onehot((key == slot.astype(F32)) & core).astype(BF)
    acc = mm(lhs, r[...])
    q[:128, :] = acc[:128].astype(BF)
    sib[:128, :] = acc[128:].astype(BF)
    tokw = mm(lhs, (cb[:, :EXPERTS].astype(F32) * rows.astype(F32)).astype(BF))
    e = iota((EXPERTS, 128), 0)
    sums = []
    for b, idv in enumerate(pair):
        tw = tokw[b * 128 : (b + 1) * 128].T
        picked = [
            jnp.sum(jnp.where(idv[k : k + 1, :] == e, tw, F32(0.0)), axis=0, keepdims=True)
            for k in range(TOP)
        ]
        sums.append(jnp.concatenate(picked, axis=0))
    q[128:, :] = hi_lo(sums[0])
    sib[128:, :] = hi_lo(sums[1])


def assemble_body(pos, comb, *refs):
    parts, (out, cg) = refs[:8], refs[8:]
    y, h = pos[0], pos[1]
    total = jnp.zeros((16, 128), F32)
    for i, off in enumerate(OFFS):
        c = lax.rem(y + (off + 4), 4) * CH
        a, b = parts[2 * i], parts[2 * i + 1]
        out[:, at(h * HALF + c, CH)] = a[:128, :]
        out[:, at((1 - h) * HALF + c, CH)] = b[:128, :]
        total = total + a[128:144, :128].astype(F32) + b[128:144, :128].astype(F32)
    cg[...] = (total[:8] + total[8:]) / comb[...].astype(F32)


def on_device(tokens, out_grad, expert_ids, combine, gate_weight, up_weight, down_weight):
    n_dp = lax.axis_size("dp")
    width = lax.axis_size("expert")
    up_ring = [(i, (i + 1) % n_dp) for i in range(n_dp)]
    down_ring = [(i, (i - 1) % n_dp) for i in range(n_dp)]
    cores = [(i, i ^ 1) for i in range(width)]
    same_core = [list(range(c, width, 2)) for c in range(2)]

    def up(x):
        return lax.ppermute(x, "dp", up_ring)

    def down(x):
        return lax.ppermute(x, "dp", down_ring)

    def swap(x):
        return lax.ppermute(x, "expert", cores)

    def exchange(x):
        n = x.shape[1]
        x = x.reshape(EXPERTS, GROUP, n)
        x = lax.all_to_all(
            x, "expert", split_axis=0, concat_axis=0, axis_index_groups=same_core, tiled=True
        )
        return x.reshape(ROWS, n)

    def spread(x):
        left, right = up(x), down(x)
        return x, left, right, up(left[:HR]), down(right[HR:])

    def spread_halves(a, b):
        la, rb, lb, ra = up(a), down(b), up(b), down(a)
        return a, b, la, lb, ra, rb, up(la), down(rb)

    tie = lax.optimization_barrier
    pos = jnp.stack([lax.axis_index("dp"), lax.axis_index("expert") & 1]).astype(I32)
    ids = expert_ids.T
    comb = combine.T
    gw, uw, dw = gate_weight[0], up_weight[0], down_weight[0]

    (pk,) = call(
        pack_body, [((272, CH), BF)], (pos, ids, comb, tokens, out_grad), name="pack"
    )
    pk = swap(pk)

    def send(weighted, rows):
        return call(
            functools.partial(send_body, weighted), [((ROWS, CH), BF)],
            (pos, ids, comb, pk, rows), name="send",
        )[0]

    xs, later = tie((send(False, tokens), pos))
    xs = exchange(xs)
    gs, xs = tie((send(True, out_grad), xs))
    gs = exchange(gs)
    (wsend,) = call(
        weight_send_body, [((3, 192, HALF), BF)], (later, gw, uw, dw), name="weight_send"
    )
    wgot = swap(wsend)
    wgu, wd = call(
        weight_join_body, [((2, UNITS, HALF), BF), ((UNITS, HALF), BF)],
        (pos, gw, uw, dw, wgot), name="weight_join",
    )
    xs, gs = spread(xs), spread_halves(gs[:HR], gs[HR:])
    (gu_a,) = call(gate_up_body, [((ROWS, 2 * UNITS), F32)], (pos, *xs, wgu), name="gate_up")
    gu_b = swap(gu_a)
    (bk_a,) = call(
        back_near_body, [((ROWS, UNITS), F32)], (pos, *gs[:6], wd), name="back_near"
    )
    (bk_a,) = call(
        back_body, [((ROWS, UNITS), F32)], (pos, bk_a, *gs[6:], wd), name="back"
    )
    bk_b = swap(bk_a)
    both, hd, cb, d2a, d2b = call(
        mid_body,
        [((ROWS, 2 * UNITS), BF), ((ROWS, UNITS), BF), ((ROWS, 128), BF)]
        + [((HR, CH), BF)] * 2,
        (pos, gu_a, gu_b, bk_a, bk_b, wgu), name="mid",
    )
    r2, q2 = up(d2a), down(d2b)
    dpa, dpb, dma, dmb, d0 = call(
        rest_body, [((HR, CH), BF)] * 4 + [((ROWS, CH), BF)], (pos, both, wgu), name="rest"
    )
    pb, ma = up(dpb), down(dma)
    pa, mb = call(pass_on_body, [((HR, CH), BF)] * 2, (pos, dpa, r2, dmb, q2), name="pass_on")
    pa, mb = up(pa), down(mb)
    pb, cb = tie((pb, cb))
    cb = exchange(cb)
    (r,) = call(finish_body, [((ROWS, CH), BF)], (pos, d0, ma, pa, mb, pb), name="finish")
    both, r, cb = tie((both, r, cb))
    r = exchange(r)
    w_own, w_other = call(
        wgrad_body, [((3, 192, HALF), BF)] * 2, (pos, both, hd, *xs, *gs),
        scratch=[pltpu.VMEM((2, UNITS, ROWS), BF), pltpu.VMEM((UNITS, ROWS), BF)],
        name="wgrad",
    )
    r, w_other = tie((r, w_other))
    qa, sib = call(
        collect_body, [((144, CH), BF)] * 2, (pos, ids, pk, r, cb), name="collect"
    )
    qb, w_other = tie((swap(sib), w_other))
    dgot = swap(w_other)
    parts = spread_halves(qa, qb)
    qb, w_own = tie((qb, w_own))
    dwg, dwu, dwd = call(
        wgrad_join_body, [((192, D), BF)] * 3, (pos, w_own, dgot), name="wgrad_join"
    )
    comb, dwg = tie((comb, dwg))
    input_grad, cg = call(
        assemble_body, [((128, D), BF), ((TOP, 128), F32)], (pos, comb, *parts), name="assemble"
    )
    return (input_grad, cg.T, dwg[None], dwu[None], dwd[None])


def solution(mesh):
    rows = P("expert", None)
    units = P("expert", "dp", None)
    return jax.shard_map(
        on_device,
        mesh=mesh,
        in_specs=(rows, rows, rows, rows, units, units, units),
        out_specs=(rows, rows, units, units, units),
        check_vma=False,
    )
```
